256 devices in a mesh: imp: 32 (over z, y_hi, core), cre: 8 (over x, y_lo).
Axes of the slice: x: 4, y: 4 (y_hi: 2, y_lo: 2; y = y_hi * 2 + y_lo), z: 8, core: 2. Of those that a mesh axis runs over, the one named last changes fastest.
Arguments:
- impressions: bfloat16 [32768, 256], P('imp'), may hold values from -24 to 24
- panels: bfloat16 [8, 2048, 256], P('cre', 'imp'), may hold values from -2 to 2
- block_lists: int32 [256, 16], P('imp'), may hold values from 0 to 127, as said below
- block_counts: int32 [256], P('imp'), may hold values from 1 to 16, as said below
- imp_weight: float32 [32768], P('imp'), may hold values from 0.2 to 5
- spend_goals: float32 [8, 2048], P('cre', 'imp'), may hold values from 0.2 to 5
- prices: float32 [8, 2048], P('cre', 'imp'), may hold values from -1 to 1
Outputs:
- final_prices: float32 [8, 2048], P('cre', 'imp')
- final_spend: float32 [8, 2048], P('cre', 'imp')
- log_norm: float32 [32768], P('imp')
The draws below stay inside these ranges and needn't reach their ends.
Inputs may be any that keep to these rules, and one draw needn't show every extreme that they name: `block_lists`: each row lists 16 different block ids; only the first block_counts entries of a row are eligible for the 128 impressions of that tile, the others must be ignored. `block_counts`: some tile has 16 eligible blocks.
All inputs are finite; a program needn't handle non-finite values.
Results may differ from the reference program's by a relative error of at most 0.0003.
Values may be sent and summed in bfloat16 or wider, within the bound.
A program may use at most 64 MiB of HBM per device.

```python
import math
import jax
import jax.numpy as jnp
from jax import lax

E = 256
IMP_DEV = 1024
CRE_LOC = 2048
TILE = 128
BLOCK = 128
MAXB = 16
ITERS = 2
CRE_GROUPS = 8
IMPS = 32768
TILES = 256
N_IMP = 32


def eligibility(key):
    block_total = CRE_GROUPS * CRE_LOC // BLOCK
    count_key = jax.random.fold_in(key, 11)
    order_key = jax.random.fold_in(key, 12)
    pick_key = jax.random.fold_in(key, 13)
    tile_counts = jax.random.randint(count_key, (TILES,), 1, MAXB + 1)
    full_tile = jax.random.randint(pick_key, (), 0, TILES)
    tile_counts = jnp.where(jnp.arange(TILES) == full_tile, MAXB, tile_counts).astype(jnp.int32)
    priority = jax.random.randint(order_key, (TILES, block_total), 0, 2 ** 16) * block_total
    priority = priority + jnp.arange(block_total)[None, :]
    tile_lists = jnp.argsort(priority, axis=1)[:, :MAXB].astype(jnp.int32)
    return (tile_lists, tile_counts)


def panel_values(key):
    value_key = jax.random.fold_in(key, 21)
    array_shape = (CRE_GROUPS, CRE_LOC, E)
    return jnp.clip(jax.random.normal(value_key, array_shape, jnp.float32), -6.0, 6.0) * E ** (-0.5)


def draw_panels(key, part):
    return panel_values(key).astype(jnp.bfloat16)


def draw_block_lists(key, part):
    tile_lists, tile_counts = eligibility(key)
    return tile_lists


def draw_block_counts(key, part):
    tile_lists, tile_counts = eligibility(key)
    return tile_counts


def draw_impressions(key, part):
    value_key = jax.random.fold_in(key, 31)
    array_shape = (IMPS, E)
    return jnp.clip(jax.random.normal(value_key, array_shape, jnp.float32), -6.0, 6.0).astype(jnp.bfloat16)


def levels(key, shape, shards, low, largest):
    def one(position, shards_of):
        heights = jax.random.uniform(jax.random.fold_in(jax.random.fold_in(key, 6), position), (shards_of,), jnp.float32, low / len(shards), largest / len(shards))
        return jnp.repeat(jnp.exp(heights), shape[position] // shards_of).reshape((-1,) + (1,) * (len(shape) - position - 1))

    loudness = one(*shards[0])
    for cut in shards[1:]:
        loudness = loudness * one(*cut)
    return loudness


def setup_inputs(seed: int = 0) -> dict:
    key_list = jax.random.split(jax.random.key(seed), 8)
    impressions = draw_impressions(jax.random.fold_in(key_list[7], 71), 0)
    panels = draw_panels(jax.random.fold_in(key_list[7], 71), 0)
    block_lists = draw_block_lists(jax.random.fold_in(key_list[7], 71), 0)
    block_counts = draw_block_counts(jax.random.fold_in(key_list[7], 71), 0)
    imp_weight = jnp.clip(jnp.exp(math.log(5.0) - 3.218876 * jax.random.uniform(key_list[4], (IMPS,), jnp.float32) ** levels(key_list[4], (IMPS,), ((0, 32),), -0.2, 0.2)), 0.2, 5.0)
    spend_goals = jnp.clip(jnp.exp(math.log(5.0) - 3.218876 * jax.random.uniform(key_list[5], (CRE_GROUPS, CRE_LOC), jnp.float32) ** levels(key_list[5], (CRE_GROUPS, CRE_LOC), ((0, 8), (1, 32)), -0.2, 0.2)), 0.2, 5.0)
    prices = jnp.clip(jax.random.uniform(key_list[6], (CRE_GROUPS, CRE_LOC), jnp.float32, -1.0, 1.0) * levels(key_list[6], (CRE_GROUPS, CRE_LOC), ((0, 8), (1, 32)), -0.4, 0.0), -1.0, 1.0)
    return dict(impressions=impressions, panels=panels, block_lists=block_lists, block_counts=block_counts, imp_weight=imp_weight, spend_goals=spend_goals, prices=prices)


NEG_FILL = -1.0e30
TAU_INV = 4.0
STEP_RATE = 0.5


def reference(impressions, panels, block_lists, block_counts, imp_weight, spend_goals, prices):
    creatives = panels.reshape(CRE_GROUPS * CRE_LOC, E)
    block_total = CRE_GROUPS * CRE_LOC // BLOCK
    col_block = jnp.arange(CRE_GROUPS * CRE_LOC, dtype=jnp.int32) // BLOCK
    block_ids = jnp.arange(block_total, dtype=jnp.int32)
    in_list = jnp.arange(MAXB, dtype=jnp.int32)[None, :] < block_counts[:, None]
    tiles_each = IMP_DEV // TILE
    imp_parts = impressions.reshape(N_IMP, IMP_DEV, E)
    list_parts = block_lists.reshape(N_IMP, tiles_each, MAXB)
    flag_parts = in_list.reshape(N_IMP, tiles_each, MAXB)
    weight_parts = imp_weight.reshape(N_IMP, IMP_DEV)
    price_vec = prices.reshape(-1)
    goal_vec = spend_goals.reshape(-1)

    def allocate(price_now):
        def one_block(spending, inputs):
            imp_rows, tile_lists, tile_flags, weights = inputs
            matches = (tile_lists[:, :, None] == block_ids[None, None, :]) & tile_flags[:, :, None]
            allowed = jnp.repeat(jnp.any(matches, axis=1), TILE, axis=0)
            col_mask = allowed[:, col_block]
            affinity = jnp.dot(imp_rows, creatives.T, preferred_element_type=jnp.float32)
            masked = jnp.where(col_mask, TAU_INV * affinity + price_now[None, :], NEG_FILL)
            row_top = jnp.max(masked, axis=1)
            row_total = jnp.sum(jnp.where(col_mask, jnp.exp(masked - row_top[:, None]), 0.0), axis=1)
            row_norm = row_top + jnp.log(row_total)
            allocation = jnp.where(col_mask, jnp.exp(masked - row_norm[:, None]), 0.0)
            return spending + jnp.sum(weights[:, None] * allocation, axis=0), row_norm

        start_spend = jnp.zeros((CRE_GROUPS * CRE_LOC,), jnp.float32)
        spending, norms = lax.scan(one_block, start_spend, (imp_parts, list_parts, flag_parts, weight_parts))
        return spending, norms.reshape(-1)

    spending = None
    norms = None
    for iteration in range(ITERS):
        spending, norms = allocate(price_vec)
        price_vec = price_vec + STEP_RATE * (jnp.log(goal_vec) - jnp.log(spending + 0.25 * goal_vec))
    return (price_vec.reshape(CRE_GROUPS, CRE_LOC), spending.reshape(CRE_GROUPS, CRE_LOC), norms)
```

```python
import functools
import math

import jax
import jax.numpy as jnp
from jax import lax
from jax.experimental import pallas as pl
from jax.experimental.pallas import tpu as pltpu
from jax.sharding import PartitionSpec as P

MESH = pl.DeviceIdType.MESH
F32 = jnp.float32
TILE = 128
NEG_FILL = -1e30
TAU_INV = 4.0
STEP_RATE = 0.5
EXP2_SCALE = TAU_INV * math.log2(math.e)


def kernel(
    n_chip,
    n_cre,
    imp_hbm,
    panel_hbm,
    list_hbm,
    count_ref,
    weight_hbm,
    goal_hbm,
    price_hbm,
    new_price_ref,
    spend_ref,
    norm_ref,
    imps,
    panels,
    kmat,
    top,
    zsum,
    bias,
    rmat,
    vcol,
    wl,
    lists,
    pg_own,
    pg,
    mx_row,
    zt_row,
    lse,
    norms,
    part1,
    part2,
    got2,
    local_sem,
    panel_send,
    right_sem,
    left_sem,
    pair_sem,
    pg_send,
    pg_recv,
    core_send,
    core_recv,
    x_send,
    x_recv,
    y_send,
    y_recv,
):
    i = lax.axis_index("imp")
    g = lax.axis_index("cre")
    c = lax.rem(i, 2)
    q = i // 2
    y = lax.rem(q, 2)
    z = q // 2
    nz = n_chip // 2
    half = nz // 2
    n_x = n_cre * 2
    me_x = g * 2 + c
    rows = imp_hbm.shape[0]
    width = panel_hbm.shape[0]
    tiles = 2 * rows // TILE
    own_tiles = tiles // 2
    packed = n_chip // 2

    def chip_peer(k):
        other = lax.rem(q + k, n_chip)
        return other, {"imp": other * 2 + c, "cre": g}

    def cre_peer(k):
        other = lax.rem(me_x + k, n_x)
        return {"imp": q * 2 + lax.rem(other, 2), "cre": other // 2}

    def z_peer(step):
        return {"imp": (lax.rem(z + step + nz, nz) * 2 + y) * 2 + c, "cre": g}

    y_peer = {"imp": (z * 2 + 1 - y) * 2 + c, "cre": g}
    core_peer = {"imp": q * 2 + 1 - c, "cre": g}

    own_rows = pl.ds(pl.multiple_of(c * rows, rows), rows)
    own_panel = pl.ds(pl.multiple_of(q * width, width), width)
    local = [
        pltpu.make_async_copy(price_hbm, pg_own.at[0], local_sem.at[0]),
        pltpu.make_async_copy(goal_hbm, pg_own.at[1], local_sem.at[1]),
        pltpu.make_async_copy(list_hbm, lists, local_sem.at[2]),
        pltpu.make_async_copy(weight_hbm, wl.at[c, pl.ds(0, own_tiles)], local_sem.at[3]),
        pltpu.make_async_copy(panel_hbm, panels.at[own_panel], local_sem.at[4]),
        pltpu.make_async_copy(imp_hbm, imps.at[own_rows], local_sem.at[5]),
    ]
    for copy in local:
        copy.start()

    barrier = pltpu.get_barrier_semaphore()
    for k in range(1, n_chip):
        pl.semaphore_signal(barrier, inc=1, device_id=chip_peer(k)[1], device_id_type=MESH)
    for k in range(1, n_x):
        pl.semaphore_signal(barrier, inc=1, device_id=cre_peer(k), device_id_type=MESH)

    for copy in local[:4]:
        copy.wait()
    pg[q] = jnp.concatenate([pg_own[0], pg_own[1]], axis=1)
    sub = lax.broadcasted_iota(jnp.int32, lists.shape, 0)
    lane = lax.broadcasted_iota(jnp.int32, lists.shape, 1)
    counts = jnp.zeros(lists.shape, jnp.int32)
    for t in range(own_tiles):
        counts = jnp.where(sub == t, count_ref[t], counts)
    wl[c, pl.ds(own_tiles, own_tiles)] = jnp.full((own_tiles, TILE), -1.0, F32)
    wl[c, pl.ds(own_tiles, own_tiles), pl.ds(0, lists.shape[1])] = jnp.where(
        lane < counts, lists[...].astype(F32), -1.0
    )

    pl.semaphore_wait(barrier, n_chip - 1 + n_x - 1)

    def panel_copy(src, slot, send, recv, peer):
        return pltpu.make_async_remote_copy(
            src_ref=src,
            dst_ref=panels.at[pl.ds(pl.multiple_of(slot * width, width), width)],
            send_sem=send,
            recv_sem=recv,
            device_id=peer,
            device_id_type=MESH,
        )

    sent = []

    def send(src, slot, recv, peer):
        copy = panel_copy(src, slot, panel_send.at[len(sent)], recv, peer)
        copy.start()
        sent.append(copy)
        return copy

    to_pair = send(panel_hbm, q, pair_sem.at[0], y_peer)
    to_right = {(0, 0): send(panel_hbm, q, right_sem.at[0, 0], z_peer(1))}
    to_left = {(0, 0): send(panel_hbm, q, left_sem.at[0, 0], z_peer(-1))}

    core_copies = [
        pltpu.make_async_remote_copy(
            src_ref=wl.at[c],
            dst_ref=wl.at[c],
            send_sem=core_send.at[0],
            recv_sem=core_recv.at[0],
            device_id=core_peer,
            device_id_type=MESH,
        ),
        pltpu.make_async_remote_copy(
            src_ref=imp_hbm,
            dst_ref=imps.at[own_rows],
            send_sem=core_send.at[1],
            recv_sem=core_recv.at[1],
            device_id=core_peer,
            device_id_type=MESH,
        ),
    ]
    for copy in core_copies:
        copy.start()
    pg_copies = []
    for k in range(1, n_chip):
        copy = pltpu.make_async_remote_copy(
            src_ref=pg.at[q],
            dst_ref=pg.at[q],
            send_sem=pg_send.at[k],
            recv_sem=pg_recv.at[q],
            device_id=chip_peer(k)[1],
            device_id_type=MESH,
        )
        copy.start()
        pg_copies.append(copy)

    core_copies[0].wait_recv()
    ids = lax.broadcasted_iota(jnp.int32, (n_chip, TILE), 0) + g * n_chip
    ids = ids.astype(F32)
    for t in range(tiles):
        row = wl[t // own_tiles, own_tiles + t % own_tiles : own_tiles + t % own_tiles + 1, :]
        hit = jnp.max(jnp.where(row == ids, 1.0, 0.0), axis=1, keepdims=True)
        bias[t] = jnp.broadcast_to(jnp.where(hit > 0.0, 0.0, NEG_FILL), (n_chip, TILE))

    for k in range(1, n_chip):
        other = lax.rem(q + k, n_chip)
        pltpu.make_async_remote_copy(
            src_ref=pg.at[q],
            dst_ref=pg.at[other],
            send_sem=pg_send.at[k],
            recv_sem=pg_recv.at[other],
            device_id=chip_peer(k)[1],
            device_id_type=MESH,
        ).wait_recv()
    low = lax.broadcasted_iota(jnp.int32, (1, TILE), 1) < width
    price_rows = []
    goal_rows = []
    for r in range(packed):
        even = pg[2 * r]
        odd = pg[2 * r + 1]
        price_rows.append(jnp.where(low, even, pltpu.roll(odd, width, 1)))
        goal_rows.append(jnp.where(low, pltpu.roll(even, width, 1), odd))
    price = jnp.concatenate(price_rows, axis=0)
    goal = jnp.concatenate(goal_rows, axis=0)

    def spread(value):
        v = jnp.exp(value)
        for r in range(packed):
            wide = jnp.broadcast_to(v[r : r + 1, :], (TILE, TILE))
            vcol[r * TILE : (r + 1) * TILE, :] = jnp.transpose(wide)
        return v

    v_lane = spread(price)

    other_shard = z * 2 + 1 - y
    to_pair_back = panel_copy(panel_hbm, other_shard, panel_send.at[0], pair_sem.at[0], y_peer)
    to_pair_back.wait_recv()

    def shard_ref(slot):
        return panels.at[pl.ds(pl.multiple_of(slot * width, width), width)]

    to_right[(0, 1)] = send(shard_ref(other_shard), other_shard, right_sem.at[0, 1], z_peer(1))
    to_left[(0, 1)] = send(shard_ref(other_shard), other_shard, left_sem.at[0, 1], z_peer(-1))

    local[4].wait()
    local[5].wait()
    core_copies[1].wait_recv()

    slab_rows = 2 * width

    def process(slabs):
        parts = []
        for zz in slabs:
            parts.append(panels[pl.ds(pl.multiple_of(zz * slab_rows, slab_rows), slab_rows), :])
        pan = parts[0] if len(parts) == 1 else jnp.concatenate(parts, axis=0)

        def body(t2, carry):
            x = imps[pl.ds(pl.multiple_of(t2 * 2 * TILE, 2 * TILE), 2 * TILE), :]
            aff = lax.dot_general(pan, x, (((1,), (1,)), ((), ())), preferred_element_type=F32)
            for n, zz in enumerate(slabs):
                for h in range(2):
                    qq = zz * 2 + h
                    at = pl.ds(pl.multiple_of(qq * width, width), width)
                    v = vcol[at, :]
                    for side in range(2):
                        t = t2 * 2 + side
                        first = n * slab_rows + h * width
                        a = aff[first : first + width, side * TILE : (side + 1) * TILE]
                        m = jnp.max(a, axis=0, keepdims=True)
                        e = jnp.exp2((a - m) * EXP2_SCALE)
                        kmat[t, at, :] = e
                        top[t, pl.ds(qq, 1), :] = TAU_INV * m
                        zsum[t, pl.ds(qq, 1), :] = jnp.sum(e * v, axis=0, keepdims=True)
            return carry

        lax.fori_loop(0, tiles // 2, body, 0)

    process([z])

    for d in range(1, half + 1):
        right_from = lax.rem(z - d + nz, nz)
        left_from = lax.rem(z + d, nz)
        for s in range(2):
            yy = y if s == 0 else 1 - y
            last = d == half
            if not last or s == 0:
                slot = right_from * 2 + yy
                panel_copy(
                    panel_hbm, slot, panel_send.at[0], right_sem.at[d - 1, s], z_peer(1)
                ).wait_recv()
                if d + 1 < half or (d + 1 == half and s == 0):
                    send(shard_ref(slot), slot, right_sem.at[d, s], z_peer(1))
            if not last or s == 1:
                slot = left_from * 2 + yy
                panel_copy(
                    panel_hbm, slot, panel_send.at[0], left_sem.at[d - 1, s], z_peer(-1)
                ).wait_recv()
                if d + 1 < half or (d + 1 == half and s == 1):
                    send(shard_ref(slot), slot, left_sem.at[d, s], z_peer(-1))
        process([right_from] if d == half else [right_from, left_from])

    def exchange_norms(phase):
        lse[phase, me_x] = mx_row[...] + jnp.log(zt_row[...])
        copies = []
        for k in range(1, n_x):
            copy = pltpu.make_async_remote_copy(
                src_ref=lse.at[phase, me_x],
                dst_ref=lse.at[phase, me_x],
                send_sem=x_send.at[phase, k],
                recv_sem=x_recv.at[phase, me_x],
                device_id=cre_peer(k),
                device_id_type=MESH,
            )
            copy.start()
            copies.append(copy)
        for k in range(1, n_x):
            other = lax.rem(me_x + k, n_x)
            pltpu.make_async_remote_copy(
                src_ref=lse.at[phase, me_x],
                dst_ref=lse.at[phase, other],
                send_sem=x_send.at[phase, k],
                recv_sem=x_recv.at[phase, other],
                device_id=cre_peer(k),
                device_id_type=MESH,
            ).wait_recv()
        most = lse[phase, 0]
        for k in range(1, n_x):
            most = jnp.maximum(most, lse[phase, k])
        total = jnp.exp(lse[phase, 0] - most)
        for k in range(1, n_x):
            total = total + jnp.exp(lse[phase, k] - most)
        norm = most + jnp.log(total)
        norms[0] = norm[:own_tiles]
        norms[1] = norm[own_tiles:]
        for t in range(tiles):
            w = wl[t // own_tiles, t % own_tiles : t % own_tiles + 1, :]
            rmat[t] = w * jnp.exp(top[t] + bias[t] - norm[t : t + 1, :])
        return copies

    def spends():
        ones = []
        for r in range(packed):

            def body(t, acc):
                k0 = kmat[t, r * TILE : r * TILE + width, :]
                k1 = kmat[t, r * TILE + width : (r + 1) * TILE, :]
                r0 = rmat[t, 2 * r : 2 * r + 1, :]
                r1 = rmat[t, 2 * r + 1 : 2 * r + 2, :]
                return (acc[0] + k0 * r0, acc[1] + k1 * r1)

            zero = jnp.zeros((width, TILE), F32)
            a0, a1 = lax.fori_loop(0, tiles, body, (zero, zero), unroll=4)
            ones.append(jnp.sum(jnp.transpose(jnp.concatenate([a0, a1], axis=0)), axis=0, keepdims=True))
        return ones

    for t in range(tiles):
        lim = top[t] + bias[t]
        m = jnp.max(lim, axis=0, keepdims=True)
        mx_row[t : t + 1, :] = m
        f = jnp.exp(lim - m)
        rmat[t] = f
        zt_row[t : t + 1, :] = jnp.sum(f * zsum[t], axis=0, keepdims=True)
    x_copies = exchange_norms(0)

    part1[q] = jnp.concatenate(spends(), axis=0) * v_lane
    y_copies = []
    for k in range(1, n_chip):
        copy = pltpu.make_async_remote_copy(
            src_ref=part1.at[q],
            dst_ref=part1.at[q],
            send_sem=y_send.at[0, k],
            recv_sem=y_recv.at[0, q],
            device_id=chip_peer(k)[1],
            device_id_type=MESH,
        )
        copy.start()
        y_copies.append(copy)
    for t in range(tiles):
        rmat[t] = jnp.exp(top[t] + bias[t] - mx_row[t : t + 1, :])
    for k in range(1, n_chip):
        other = lax.rem(q + k, n_chip)
        pltpu.make_async_remote_copy(
            src_ref=part1.at[q],
            dst_ref=part1.at[other],
            send_sem=y_send.at[0, k],
            recv_sem=y_recv.at[0, other],
            device_id=chip_peer(k)[1],
            device_id_type=MESH,
        ).wait_recv()
    spend = part1[0]
    for k in range(1, n_chip):
        spend = spend + part1[k]
    price = price + STEP_RATE * (jnp.log(goal) - jnp.log(spend + 0.25 * goal))
    v_lane = spread(price)

    def zbody(t, carry):
        acc = jnp.zeros((8, TILE), F32)
        for qq in range(n_chip):
            part = kmat[t, qq * width : (qq + 1) * width, :] * vcol[qq * width : (qq + 1) * width, :]
            acc = acc + jnp.sum(part.reshape(width // 8, 8, TILE), axis=0) * rmat[t, qq : qq + 1, :]
        zt_row[pl.ds(t, 1), :] = jnp.sum(acc, axis=0, keepdims=True)
        return carry

    lax.fori_loop(0, tiles, zbody, 0)
    x_copies += exchange_norms(1)

    for r, value in enumerate(spends()):
        part2[r] = value * v_lane[r : r + 1, :]
    for k in range(1, n_chip):
        other, peer = chip_peer(k)
        copy = pltpu.make_async_remote_copy(
            src_ref=part2.at[other // 2],
            dst_ref=got2.at[q],
            send_sem=y_send.at[1, k],
            recv_sem=y_recv.at[1, q],
            device_id=peer,
            device_id_type=MESH,
        )
        copy.start()
        y_copies.append(copy)
    got2[q] = part2[q // 2]
    norm_ref[...] = norms[c]
    for k in range(1, n_chip):
        other = lax.rem(q + k, n_chip)
        pltpu.make_async_remote_copy(
            src_ref=part2.at[0],
            dst_ref=got2.at[other],
            send_sem=y_send.at[1, k],
            recv_sem=y_recv.at[1, other],
            device_id=chip_peer(k)[1],
            device_id_type=MESH,
        ).wait_recv()
    spend = got2[0]
    for k in range(1, n_chip):
        spend = spend + got2[k]

    row = lax.broadcasted_iota(jnp.int32, (packed, TILE), 0)

    def own_half(value):
        return jnp.where(y == 0, value, pltpu.roll(value, width, 1))[:, :width]

    price_row = jnp.sum(jnp.where(row == z, price, 0.0), axis=0, keepdims=True)
    goal_row = jnp.sum(jnp.where(row == z, goal, 0.0), axis=0, keepdims=True)
    final = price_row + STEP_RATE * (jnp.log(goal_row) - jnp.log(spend + 0.25 * goal_row))
    spend_ref[...] = own_half(spend)
    new_price_ref[...] = own_half(final)

    for copy in sent + core_copies + pg_copies + x_copies + y_copies:
        copy.wait_send()


def solution(mesh):
    n_chip = mesh.shape["imp"] // 2
    n_cre = mesh.shape["cre"]
    half = n_chip // 4

    def step(impressions, panels, block_lists, block_counts, imp_weight, spend_goals, prices):
        rows, wide = impressions.shape
        width = panels.shape[1]
        own_tiles = rows // TILE
        tiles = 2 * own_tiles
        n_x = n_cre * 2
        creatives = n_chip * width
        any_spec = pl.BlockSpec(memory_space=pl.ANY)
        vmem = pl.BlockSpec(memory_space=pltpu.VMEM)
        dma = pltpu.SemaphoreType.DMA
        new_prices, spend, norms = pl.pallas_call(
            functools.partial(kernel, n_chip, n_cre),
            out_shape=(
                jax.ShapeDtypeStruct((1, width), F32),
                jax.ShapeDtypeStruct((1, width), F32),
                jax.ShapeDtypeStruct((own_tiles, TILE), F32),
            ),
            in_specs=[
                any_spec,
                any_spec,
                any_spec,
                pl.BlockSpec(memory_space=pltpu.SMEM),
                any_spec,
                any_spec,
                any_spec,
            ],
            out_specs=(vmem, vmem, vmem),
            scratch_shapes=[
                pltpu.VMEM((2 * rows, wide), jnp.bfloat16),
                pltpu.VMEM((creatives, wide), jnp.bfloat16),
                pltpu.VMEM((tiles, creatives, TILE), F32),
                pltpu.VMEM((tiles, n_chip, TILE), F32),
                pltpu.VMEM((tiles, n_chip, TILE), F32),
                pltpu.VMEM((tiles, n_chip, TILE), F32),
                pltpu.VMEM((tiles, n_chip, TILE), F32),
                pltpu.VMEM((creatives, TILE), F32),
                pltpu.VMEM((2, tiles, TILE), F32),
                pltpu.VMEM((own_tiles, block_lists.shape[1]), jnp.int32),
                pltpu.VMEM((2, 1, width), F32),
                pltpu.VMEM((n_chip, 1, TILE), F32),
                pltpu.VMEM((tiles, TILE), F32),
                pltpu.VMEM((tiles, TILE), F32),
                pltpu.VMEM((2, n_x, tiles, TILE), F32),
                pltpu.VMEM((2, own_tiles, TILE), F32),
                pltpu.VMEM((n_chip, n_chip // 2, TILE), F32),
                pltpu.VMEM((n_chip // 2, 1, TILE), F32),
                pltpu.VMEM((n_chip, 1, TILE), F32),
                dma((6,)),
                dma((4 * half + 1,)),
                dma((half, 2)),
                dma((half, 2)),
                dma((1,)),
                dma((n_chip,)),
                dma((n_chip,)),
                dma((2,)),
                dma((2,)),
                dma((2, n_x)),
                dma((2, n_x)),
                dma((2, n_chip)),
                dma((2, n_chip)),
            ],
            compiler_params=pltpu.CompilerParams(
                collective_id=0, has_side_effects=True, vmem_limit_bytes=40 << 20
            ),
        )(
            impressions,
            panels.reshape(width, wide),
            block_lists,
            block_counts,
            imp_weight.reshape(own_tiles, TILE),
            spend_goals,
            prices,
        )
        return new_prices, spend, norms.reshape(rows)

    return jax.shard_map(
        step,
        mesh=mesh,
        in_specs=(
            P("imp", None),
            P("cre", "imp", None),
            P("imp", None),
            P("imp"),
            P("imp"),
            P("cre", "imp"),
            P("cre", "imp"),
        ),
        out_specs=(P("cre", "imp"), P("cre", "imp"), P("imp")),
        check_vma=False,
    )
```

```python
import functools
import math

import jax
import jax.numpy as jnp
from jax import lax
from jax.experimental import pallas as pl
from jax.experimental.pallas import tpu as pltpu
from jax.sharding import PartitionSpec as P

MESH = pl.DeviceIdType.MESH
F32 = jnp.float32
TILE = 128
NEG_FILL = -1e30
TAU_INV = 4.0
STEP_RATE = 0.5
EXP2_SCALE = TAU_INV * math.log2(math.e)


def kernel(
    n_chip,
    n_cre,
    imp_hbm,
    panel_hbm,
    list_hbm,
    count_ref,
    weight_hbm,
    goal_hbm,
    price_hbm,
    new_price_ref,
    spend_ref,
    norm_ref,
    imps,
    panels,
    kmat,
    top,
    zsum,
    bias,
    rmat,
    vcol,
    wl,
    lists,
    pg_own,
    pg,
    mx_row,
    zt_row,
    lse,
    norms,
    part1,
    part2,
    got2,
    local_sem,
    panel_send,
    panel_recv,
    pg_send,
    pg_recv,
    core_send,
    core_recv,
    x_send,
    x_recv,
    y_send,
    y_recv,
):
    i = lax.axis_index("imp")
    g = lax.axis_index("cre")
    c = lax.rem(i, 2)
    q = i // 2
    y = lax.rem(q, 2)
    z = q // 2
    nz = n_chip // 2
    half = nz // 2
    n_x = n_cre * 2
    me_x = g * 2 + c
    rows = imp_hbm.shape[0]
    width = panel_hbm.shape[0]
    tiles = 2 * rows // TILE
    own_tiles = tiles // 2
    packed = n_chip // 2

    mirror = g + 1 - 2 * lax.rem(g, 2)

    def plane(step):
        return lax.rem(z + step + nz, nz)

    def slot_of(step, dy):
        return plane(step) * 2 + (y if dy == 0 else 1 - y)

    def at(step, dy):
        return {"imp": slot_of(step, dy) * 2 + c, "cre": g if dy == 0 else mirror}

    chips = [(half, 1), (half, 0)]
    for d in range(half - 1, 0, -1):
        chips += [(d, 1), (-d, 1), (d, 0), (-d, 0)]
    chips += [(0, 1)]

    def cre_peer(k):
        other = lax.rem(me_x + k, n_x)
        return {"imp": q * 2 + lax.rem(other, 2), "cre": other // 2}

    far_first = sorted(range(1, n_x), key=lambda k: -min(k, n_x - k))
    core_peer = {"imp": q * 2 + 1 - c, "cre": g}

    barrier = pltpu.get_barrier_semaphore()
    for step, dy in chips:
        pl.semaphore_signal(barrier, inc=1, device_id=at(step, dy), device_id_type=MESH)
    for k in far_first:
        pl.semaphore_signal(barrier, inc=1, device_id=cre_peer(k), device_id_type=MESH)

    own_rows = pl.ds(pl.multiple_of(c * rows, rows), rows)

    def shard_ref(slot):
        return panels.at[pl.ds(pl.multiple_of(slot * width, width), width)]

    local = [
        pltpu.make_async_copy(price_hbm, pg_own.at[0], local_sem.at[0]),
        pltpu.make_async_copy(goal_hbm, pg_own.at[1], local_sem.at[1]),
        pltpu.make_async_copy(list_hbm, lists, local_sem.at[2]),
        pltpu.make_async_copy(weight_hbm, wl.at[c, pl.ds(0, own_tiles)], local_sem.at[3]),
        pltpu.make_async_copy(panel_hbm, shard_ref(q), local_sem.at[4]),
        pltpu.make_async_copy(imp_hbm, imps.at[own_rows], local_sem.at[5]),
    ]
    for copy in local:
        copy.start()

    pl.semaphore_wait(barrier, n_chip - 1 + n_x - 1)

    sent = []

    def panel_copy(src, slot, peer, n=0):
        return pltpu.make_async_remote_copy(
            src_ref=src,
            dst_ref=shard_ref(slot),
            send_sem=panel_send.at[n],
            recv_sem=panel_recv.at[slot],
            device_id=peer,
            device_id_type=MESH,
        )

    def send(src, slot, peer):
        copy = panel_copy(src, slot, peer, len(sent))
        copy.start()
        sent.append(copy)

    def arrived(step, dy):
        panel_copy(panel_hbm, slot_of(step, dy), at(0, 1)).wait_recv()

    for step in (2, -2, 1, -1):
        for dy in (1, 0):
            send(panel_hbm, q, at(step, dy))
    send(panel_hbm, q, at(0, 1))

    imp_copy = pltpu.make_async_remote_copy(
        src_ref=imp_hbm,
        dst_ref=imps.at[own_rows],
        send_sem=core_send.at[1],
        recv_sem=core_recv.at[1],
        device_id=core_peer,
        device_id_type=MESH,
    )
    imp_copy.start()

    for copy in local[:2]:
        copy.wait()
    pg[q] = jnp.concatenate([pg_own[0], pg_own[1]], axis=1)
    pg_copies = []

    def pg_copy(k, slot):
        return pltpu.make_async_remote_copy(
            src_ref=pg.at[q],
            dst_ref=pg.at[slot],
            send_sem=pg_send.at[k],
            recv_sem=pg_recv.at[slot],
            device_id=at(*chips[k]),
            device_id_type=MESH,
        )

    for k in range(n_chip - 1):
        copy = pg_copy(k, q)
        copy.start()
        pg_copies.append(copy)

    for copy in local[2:4]:
        copy.wait()
    sub = lax.broadcasted_iota(jnp.int32, lists.shape, 0)
    lane = lax.broadcasted_iota(jnp.int32, lists.shape, 1)
    counts = jnp.zeros(lists.shape, jnp.int32)
    for t in range(own_tiles):
        counts = jnp.where(sub == t, count_ref[t], counts)
    wl[c, pl.ds(own_tiles, own_tiles)] = jnp.full((own_tiles, TILE), -1.0, F32)
    wl[c, pl.ds(own_tiles, own_tiles), pl.ds(0, lists.shape[1])] = jnp.where(
        lane < counts, lists[...].astype(F32), -1.0
    )
    wl_copy = pltpu.make_async_remote_copy(
        src_ref=wl.at[c],
        dst_ref=wl.at[c],
        send_sem=core_send.at[0],
        recv_sem=core_recv.at[0],
        device_id=core_peer,
        device_id_type=MESH,
    )
    wl_copy.start()
    core_copies = [wl_copy, imp_copy]

    wl_copy.wait_recv()
    ids = lax.broadcasted_iota(jnp.int32, (n_chip, TILE), 0)
    ids = ids + jnp.where(lax.rem(ids, 2) == y, g, mirror) * n_chip
    ids = ids.astype(F32)
    for t in range(tiles):
        row = wl[t // own_tiles, own_tiles + t % own_tiles : own_tiles + t % own_tiles + 1, :]
        hit = jnp.max(jnp.where(row == ids, 1.0, 0.0), axis=1, keepdims=True)
        bias[t] = jnp.broadcast_to(jnp.where(hit > 0.0, 0.0, NEG_FILL), (n_chip, TILE))

    for sign in (1, -1):
        for s in range(2):
            dy = s if sign == 1 else 1 - s
            slot = slot_of(-2 * sign, dy)
            arrived(-2 * sign, dy)
            if s == 0:
                send(shard_ref(slot), slot, at(2 * sign, 0))
            send(shard_ref(slot), slot, at(sign, 0))

    for k in range(n_chip - 1):
        pg_copy(k, slot_of(*chips[k])).wait_recv()
    low = lax.broadcasted_iota(jnp.int32, (1, TILE), 1) < width
    price_rows = []
    goal_rows = []
    for r in range(packed):
        even = pg[2 * r]
        odd = pg[2 * r + 1]
        price_rows.append(jnp.where(low, even, pltpu.roll(odd, width, 1)))
        goal_rows.append(jnp.where(low, pltpu.roll(even, width, 1), odd))
    price = jnp.concatenate(price_rows, axis=0)
    goal = jnp.concatenate(goal_rows, axis=0)

    def spread(value):
        v = jnp.exp(value)
        for r in range(packed):
            wide = jnp.broadcast_to(v[r : r + 1, :], (TILE, TILE))
            vcol[r * TILE : (r + 1) * TILE, :] = jnp.transpose(wide)
        return v

    v_lane = spread(price)

    slab_rows = 2 * width

    def process(slabs):
        parts = []
        for zz in slabs:
            parts.append(panels[pl.ds(pl.multiple_of(zz * slab_rows, slab_rows), slab_rows), :])
        pan = parts[0] if len(parts) == 1 else jnp.concatenate(parts, axis=0)

        def body(t2, carry):
            x = imps[pl.ds(pl.multiple_of(t2 * 2 * TILE, 2 * TILE), 2 * TILE), :]
            aff = lax.dot_general(pan, x, (((1,), (1,)), ((), ())), preferred_element_type=F32)
            for n, zz in enumerate(slabs):
                for h in range(2):
                    qq = zz * 2 + h
                    place = pl.ds(pl.multiple_of(qq * width, width), width)
                    v = vcol[place, :]
                    for side in range(2):
                        t = t2 * 2 + side
                        first = n * slab_rows + h * width
                        a = aff[first : first + width, side * TILE : (side + 1) * TILE]
                        m = jnp.max(a, axis=0, keepdims=True)
                        e = jnp.exp2((a - m) * EXP2_SCALE)
                        kmat[t, place, :] = e
                        top[t, pl.ds(qq, 1), :] = TAU_INV * m
                        zsum[t, pl.ds(qq, 1), :] = jnp.sum(e * v, axis=0, keepdims=True)
            return carry

        lax.fori_loop(0, tiles // 2, body, 0, unroll=8)

    for copy in local[4:]:
        copy.wait()
    imp_copy.wait_recv()
    arrived(0, 1)
    process([z])
    for d in range(1, half):
        for step in (d, -d):
            for dy in range(2):
                if d != 2:
                    arrived(step, dy)
        process([plane(d), plane(-d)])
    for dy in range(2):
        arrived(half, dy)
    process([plane(half)])

    def exchange_norms(phase):
        lse[phase, me_x] = mx_row[...] + jnp.log(zt_row[...])
        copies = []
        for k in far_first:
            copy = pltpu.make_async_remote_copy(
                src_ref=lse.at[phase, me_x],
                dst_ref=lse.at[phase, me_x],
                send_sem=x_send.at[phase, k],
                recv_sem=x_recv.at[phase, me_x],
                device_id=cre_peer(k),
                device_id_type=MESH,
            )
            copy.start()
            copies.append(copy)
        for k in range(1, n_x):
            other = lax.rem(me_x + k, n_x)
            pltpu.make_async_remote_copy(
                src_ref=lse.at[phase, me_x],
                dst_ref=lse.at[phase, other],
                send_sem=x_send.at[phase, k],
                recv_sem=x_recv.at[phase, other],
                device_id=cre_peer(k),
                device_id_type=MESH,
            ).wait_recv()
        most = lse[phase, 0]
        for k in range(1, n_x):
            most = jnp.maximum(most, lse[phase, k])
        total = jnp.exp(lse[phase, 0] - most)
        for k in range(1, n_x):
            total = total + jnp.exp(lse[phase, k] - most)
        norm = most + jnp.log(total)
        norms[0] = norm[:own_tiles]
        norms[1] = norm[own_tiles:]
        for t in range(tiles):
            w = wl[t // own_tiles, t % own_tiles : t % own_tiles + 1, :]
            rmat[t] = w * jnp.exp(top[t] + bias[t] - norm[t : t + 1, :])
        return copies

    def spends():
        ones = []
        for r in range(packed):

            def body(t, acc):
                k0 = kmat[t, r * TILE : r * TILE + width, :]
                k1 = kmat[t, r * TILE + width : (r + 1) * TILE, :]
                r0 = rmat[t, 2 * r : 2 * r + 1, :]
                r1 = rmat[t, 2 * r + 1 : 2 * r + 2, :]
                return (acc[0] + k0 * r0, acc[1] + k1 * r1)

            zero = jnp.zeros((width, TILE), F32)
            a0, a1 = lax.fori_loop(0, tiles, body, (zero, zero), unroll=4)
            ones.append(jnp.sum(jnp.transpose(jnp.concatenate([a0, a1], axis=0)), axis=0, keepdims=True))
        return ones

    for t in range(tiles):
        lim = top[t] + bias[t]
        m = jnp.max(lim, axis=0, keepdims=True)
        mx_row[t : t + 1, :] = m
        f = jnp.exp(lim - m)
        rmat[t] = f
        zt_row[t : t + 1, :] = jnp.sum(f * zsum[t], axis=0, keepdims=True)
    x_copies = exchange_norms(0)

    part1[q] = jnp.concatenate(spends(), axis=0) * v_lane
    y_copies = []
    for k in range(n_chip - 1):
        copy = pltpu.make_async_remote_copy(
            src_ref=part1.at[q],
            dst_ref=part1.at[q],
            send_sem=y_send.at[0, k],
            recv_sem=y_recv.at[0, q],
            device_id=at(*chips[k]),
            device_id_type=MESH,
        )
        copy.start()
        y_copies.append(copy)
    for t in range(tiles):
        rmat[t] = jnp.exp(top[t] + bias[t] - mx_row[t : t + 1, :])
    for k in range(n_chip - 1):
        other = slot_of(*chips[k])
        pltpu.make_async_remote_copy(
            src_ref=part1.at[q],
            dst_ref=part1.at[other],
            send_sem=y_send.at[0, k],
            recv_sem=y_recv.at[0, other],
            device_id=at(*chips[k]),
            device_id_type=MESH,
        ).wait_recv()
    spend = part1[0]
    for k in range(1, n_chip):
        spend = spend + part1[k]
    price = price + STEP_RATE * (jnp.log(goal) - jnp.log(spend + 0.25 * goal))
    v_lane = spread(price)

    def zbody(t, carry):
        acc = jnp.zeros((8, TILE), F32)
        for qq in range(n_chip):
            part = kmat[t, qq * width : (qq + 1) * width, :] * vcol[qq * width : (qq + 1) * width, :]
            acc = acc + jnp.sum(part.reshape(width // 8, 8, TILE), axis=0) * rmat[t, qq : qq + 1, :]
        zt_row[pl.ds(t, 1), :] = jnp.sum(acc, axis=0, keepdims=True)
        return carry

    lax.fori_loop(0, tiles, zbody, 0)
    x_copies += exchange_norms(1)

    for r, value in enumerate(spends()):
        part2[r] = value * v_lane[r : r + 1, :]
    for k in range(n_chip - 1):
        other, peer = slot_of(*chips[k]), at(*chips[k])
        copy = pltpu.make_async_remote_copy(
            src_ref=part2.at[other // 2],
            dst_ref=got2.at[q],
            send_sem=y_send.at[1, k],
            recv_sem=y_recv.at[1, q],
            device_id=peer,
            device_id_type=MESH,
        )
        copy.start()
        y_copies.append(copy)
    got2[q] = part2[q // 2]
    norm_ref[...] = norms[c]
    for k in range(n_chip - 1):
        other = slot_of(*chips[k])
        pltpu.make_async_remote_copy(
            src_ref=part2.at[0],
            dst_ref=got2.at[other],
            send_sem=y_send.at[1, k],
            recv_sem=y_recv.at[1, other],
            device_id=at(*chips[k]),
            device_id_type=MESH,
        ).wait_recv()
    spend = got2[0]
    for k in range(1, n_chip):
        spend = spend + got2[k]

    row = lax.broadcasted_iota(jnp.int32, (packed, TILE), 0)

    def own_half(value):
        return jnp.where(y == 0, value, pltpu.roll(value, width, 1))[:, :width]

    price_row = jnp.sum(jnp.where(row == z, price, 0.0), axis=0, keepdims=True)
    goal_row = jnp.sum(jnp.where(row == z, goal, 0.0), axis=0, keepdims=True)
    final = price_row + STEP_RATE * (jnp.log(goal_row) - jnp.log(spend + 0.25 * goal_row))
    spend_ref[...] = own_half(spend)
    new_price_ref[...] = own_half(final)

    for copy in sent + core_copies + pg_copies + x_copies + y_copies:
        copy.wait_send()


def solution(mesh):
    n_chip = mesh.shape["imp"] // 2
    n_cre = mesh.shape["cre"]
    half = n_chip // 4

    def step(impressions, panels, block_lists, block_counts, imp_weight, spend_goals, prices):
        rows, wide = impressions.shape
        width = panels.shape[1]
        own_tiles = rows // TILE
        tiles = 2 * own_tiles
        n_x = n_cre * 2
        creatives = n_chip * width
        any_spec = pl.BlockSpec(memory_space=pl.ANY)
        vmem = pl.BlockSpec(memory_space=pltpu.VMEM)
        dma = pltpu.SemaphoreType.DMA
        new_prices, spend, norms = pl.pallas_call(
            functools.partial(kernel, n_chip, n_cre),
            out_shape=(
                jax.ShapeDtypeStruct((1, width), F32),
                jax.ShapeDtypeStruct((1, width), F32),
                jax.ShapeDtypeStruct((own_tiles, TILE), F32),
            ),
            in_specs=[
                any_spec,
                any_spec,
                any_spec,
                pl.BlockSpec(memory_space=pltpu.SMEM),
                any_spec,
                any_spec,
                any_spec,
            ],
            out_specs=(vmem, vmem, vmem),
            scratch_shapes=[
                pltpu.VMEM((2 * rows, wide), jnp.bfloat16),
                pltpu.VMEM((creatives, wide), jnp.bfloat16),
                pltpu.VMEM((tiles, creatives, TILE), F32),
                pltpu.VMEM((tiles, n_chip, TILE), F32),
                pltpu.VMEM((tiles, n_chip, TILE), F32),
                pltpu.VMEM((tiles, n_chip, TILE), F32),
                pltpu.VMEM((tiles, n_chip, TILE), F32),
                pltpu.VMEM((creatives, TILE), F32),
                pltpu.VMEM((2, tiles, TILE), F32),
                pltpu.VMEM((own_tiles, block_lists.shape[1]), jnp.int32),
                pltpu.VMEM((2, 1, width), F32),
                pltpu.VMEM((n_chip, 1, TILE), F32),
                pltpu.VMEM((tiles, TILE), F32),
                pltpu.VMEM((tiles, TILE), F32),
                pltpu.VMEM((2, n_x, tiles, TILE), F32),
                pltpu.VMEM((2, own_tiles, TILE), F32),
                pltpu.VMEM((n_chip, n_chip // 2, TILE), F32),
                pltpu.VMEM((n_chip // 2, 1, TILE), F32),
                pltpu.VMEM((n_chip, 1, TILE), F32),
                dma((6,)),
                dma((n_chip - 1,)),
                dma((n_chip,)),
                dma((n_chip,)),
                dma((n_chip,)),
                dma((2,)),
                dma((2,)),
                dma((2, n_x)),
                dma((2, n_x)),
                dma((2, n_chip)),
                dma((2, n_chip)),
            ],
            compiler_params=pltpu.CompilerParams(
                collective_id=0, has_side_effects=True, vmem_limit_bytes=63 << 20
            ),
        )(
            impressions,
            panels.reshape(width, wide),
            block_lists,
            block_counts,
            imp_weight.reshape(own_tiles, TILE),
            spend_goals,
            prices,
        )
        return new_prices, spend, norms.reshape(rows)

    return jax.shard_map(
        step,
        mesh=mesh,
        in_specs=(
            P("imp", None),
            P("cre", "imp", None),
            P("imp", None),
            P("imp"),
            P("imp"),
            P("cre", "imp"),
            P("cre", "imp"),
        ),
        out_specs=(P("cre", "imp"), P("cre", "imp"), P("imp")),
        check_vma=False,
    )
```

```python
import functools
import math

import jax
import jax.numpy as jnp
from jax import lax
from jax.experimental import pallas as pl
from jax.experimental.pallas import tpu as pltpu
from jax.sharding import PartitionSpec as P

MESH = pl.DeviceIdType.MESH
F32 = jnp.float32
TILE = 128
NEG_FILL = -1e30
TAU_INV = 4.0
STEP_RATE = 0.5
EXP2_SCALE = TAU_INV * math.log2(math.e)


def kernel(
    n_chip,
    n_cre,
    imp_hbm,
    panel_hbm,
    list_hbm,
    count_ref,
    weight_hbm,
    goal_hbm,
    price_hbm,
    spend_ref,
    norm_ref,
    imps,
    panels,
    kmat,
    top,
    zsum,
    bias,
    factor,
    grow,
    vcol,
    wl,
    lists,
    pg_own,
    pg,
    mx_row,
    zt_row,
    lse,
    norms,
    part1,
    part2,
    got2,
    local_sem,
    panel_send,
    panel_recv,
    pg_send,
    pg_recv,
    core_send,
    core_recv,
    x_send,
    x_recv,
    y_send,
    y_recv,
):
    i = lax.axis_index("imp")
    g = lax.axis_index("cre")
    c = lax.rem(i, 2)
    q = i // 2
    y = lax.rem(q, 2)
    z = q // 2
    nz = n_chip // 2
    half = nz // 2
    n_x = n_cre * 2
    me_x = g * 2 + c
    rows = imp_hbm.shape[0]
    width = panel_hbm.shape[0]
    tiles = 2 * rows // TILE
    own_tiles = tiles // 2
    packed = n_chip // 2

    mirror = g + 1 - 2 * lax.rem(g, 2)

    def plane(step):
        return lax.rem(z + step + nz, nz)

    def slot_of(step, dy):
        return plane(step) * 2 + (y if dy == 0 else 1 - y)

    def at(step, dy):
        return {"imp": slot_of(step, dy) * 2 + c, "cre": g if dy == 0 else mirror}

    chips = [(half, 1), (half, 0)]
    for d in range(half - 1, 0, -1):
        chips += [(d, 1), (-d, 1), (d, 0), (-d, 0)]
    chips += [(0, 1)]

    def cre_peer(k):
        other = lax.rem(me_x + k, n_x)
        return {"imp": q * 2 + lax.rem(other, 2), "cre": other // 2}

    far_first = sorted(range(1, n_x), key=lambda k: -min(k, n_x - k))
    core_peer = {"imp": q * 2 + 1 - c, "cre": g}

    barrier = pltpu.get_barrier_semaphore()
    near = [(step, dy) for step, dy in chips if abs(step) <= 2]
    for step, dy in near:
        pl.semaphore_signal(barrier, inc=1, device_id=at(step, dy), device_id_type=MESH)
    for k in far_first:
        pl.semaphore_signal(barrier, inc=1, device_id=cre_peer(k), device_id_type=MESH)

    own_rows = pl.ds(pl.multiple_of(c * rows, rows), rows)

    def shard_ref(slot):
        return panels.at[pl.ds(pl.multiple_of(slot * width, width), width)]

    local = [
        pltpu.make_async_copy(price_hbm, pg_own.at[0], local_sem.at[0]),
        pltpu.make_async_copy(goal_hbm, pg_own.at[1], local_sem.at[1]),
        pltpu.make_async_copy(list_hbm, lists, local_sem.at[2]),
        pltpu.make_async_copy(weight_hbm, wl.at[c, pl.ds(0, own_tiles)], local_sem.at[3]),
        pltpu.make_async_copy(panel_hbm, shard_ref(q), local_sem.at[4]),
        pltpu.make_async_copy(imp_hbm, imps.at[own_rows], local_sem.at[5]),
    ]
    for copy in local:
        copy.start()

    for copy in local[:2]:
        copy.wait()
    pg[q] = jnp.concatenate([pg_own[0], pg_own[1]], axis=1)
    pl.semaphore_wait(barrier, len(near) + n_x - 1)

    pg_copies = []

    def pg_copy(slot, peer, n=0):
        return pltpu.make_async_remote_copy(
            src_ref=pg.at[slot],
            dst_ref=pg.at[slot],
            send_sem=pg_send.at[n],
            recv_sem=pg_recv.at[slot],
            device_id=peer,
            device_id_type=MESH,
        )

    def pg_put(slot, peer):
        copy = pg_copy(slot, peer, len(pg_copies))
        copy.start()
        pg_copies.append(copy)

    def pg_arrived(step, dy):
        pg_copy(slot_of(step, dy), at(0, 1)).wait_recv()

    for step, dy in near:
        pg_put(q, at(step, dy))

    sent = []

    def panel_copy(src, slot, peer, n=0):
        return pltpu.make_async_remote_copy(
            src_ref=src,
            dst_ref=shard_ref(slot),
            send_sem=panel_send.at[n],
            recv_sem=panel_recv.at[slot],
            device_id=peer,
            device_id_type=MESH,
        )

    def send(src, slot, peer):
        copy = panel_copy(src, slot, peer, len(sent))
        copy.start()
        sent.append(copy)

    def arrived(step, dy):
        panel_copy(panel_hbm, slot_of(step, dy), at(0, 1)).wait_recv()

    for step in (2, -2, 1, -1):
        for dy in (1, 0):
            send(panel_hbm, q, at(step, dy))
    send(panel_hbm, q, at(0, 1))

    imp_copy = pltpu.make_async_remote_copy(
        src_ref=imp_hbm,
        dst_ref=imps.at[own_rows],
        send_sem=core_send.at[1],
        recv_sem=core_recv.at[1],
        device_id=core_peer,
        device_id_type=MESH,
    )
    imp_copy.start()

    for copy in local[2:4]:
        copy.wait()
    sub = lax.broadcasted_iota(jnp.int32, lists.shape, 0)
    lane = lax.broadcasted_iota(jnp.int32, lists.shape, 1)
    counts = jnp.zeros(lists.shape, jnp.int32)
    for t in range(own_tiles):
        counts = jnp.where(sub == t, count_ref[t], counts)
    wl[c, pl.ds(own_tiles, own_tiles)] = jnp.full((own_tiles, TILE), -1.0, F32)
    wl[c, pl.ds(own_tiles, own_tiles), pl.ds(0, lists.shape[1])] = jnp.where(
        lane < counts, lists[...].astype(F32), -1.0
    )
    wl_copy = pltpu.make_async_remote_copy(
        src_ref=wl.at[c],
        dst_ref=wl.at[c],
        send_sem=core_send.at[0],
        recv_sem=core_recv.at[0],
        device_id=core_peer,
        device_id_type=MESH,
    )
    wl_copy.start()
    core_copies = [wl_copy, imp_copy]

    wl_copy.wait_recv()
    ids = lax.broadcasted_iota(jnp.int32, (n_chip, TILE), 0)
    ids = ids + jnp.where(lax.rem(ids, 2) == y, g, mirror) * n_chip
    ids = ids.astype(F32)
    for t in range(tiles):
        row = wl[t // own_tiles, own_tiles + t % own_tiles : own_tiles + t % own_tiles + 1, :]
        hit = jnp.max(jnp.where(row == ids, 1.0, 0.0), axis=1, keepdims=True)
        level = jnp.broadcast_to(jnp.where(hit > 0.0, 0.0, NEG_FILL), (n_chip, TILE))
        for b in range(n_chip):
            bias[t, b] = jnp.broadcast_to(level[b : b + 1, :], (8, TILE))

    for sign in (1, -1):
        for s in range(2):
            dy = s if sign == 1 else 1 - s
            slot = slot_of(-2 * sign, dy)
            pg_arrived(-2 * sign, dy)
            if s == 0:
                pg_put(slot, at(2 * sign, 0))
            pg_put(slot, at(sign, 0))
            arrived(-2 * sign, dy)
            if s == 0:
                send(shard_ref(slot), slot, at(2 * sign, 0))
            send(shard_ref(slot), slot, at(sign, 0))

    low = lax.broadcasted_iota(jnp.int32, (1, TILE), 1) < width
    def spread(value):
        v = jnp.exp(value)
        for r in range(packed):
            wide = jnp.broadcast_to(v[r : r + 1, :], (TILE, TILE))
            vcol[r * TILE : (r + 1) * TILE, :] = jnp.transpose(wide)
        return v

    def spread_slab(zz):
        row = jnp.where(low, pg[2 * zz], pltpu.roll(pg[2 * zz + 1], width, 1))
        wide = jnp.broadcast_to(jnp.exp(row), (TILE, TILE))
        vcol[pl.ds(pl.multiple_of(zz * TILE, TILE), TILE), :] = jnp.transpose(wide)

    slab_rows = 2 * width

    def process(slabs):
        parts = []
        for zz in slabs:
            parts.append(panels[pl.ds(pl.multiple_of(zz * slab_rows, slab_rows), slab_rows), :])
        pan = parts[0] if len(parts) == 1 else jnp.concatenate(parts, axis=0)

        def body(t2, carry):
            x = imps[pl.ds(pl.multiple_of(t2 * 2 * TILE, 2 * TILE), 2 * TILE), :]
            aff = lax.dot_general(pan, x, (((1,), (1,)), ((), ())), preferred_element_type=F32)
            for n, zz in enumerate(slabs):
                for h in range(2):
                    qq = zz * 2 + h
                    place = pl.ds(pl.multiple_of(qq * width, width), width)
                    v = vcol[place, :].reshape(width // 8, 8, TILE)
                    for side in range(2):
                        t = t2 * 2 + side
                        first = n * slab_rows + h * width
                        a = aff[first : first + width, side * TILE : (side + 1) * TILE]
                        a = a.reshape(width // 8, 8, TILE)
                        m = jnp.max(a, axis=0)
                        e = jnp.exp2((a - m) * EXP2_SCALE)
                        kmat[t, place, :] = e.reshape(width, TILE)
                        top[t, qq] = TAU_INV * m + bias[t, qq]
                        zsum[t, qq] = jnp.sum(e * v, axis=0)
            return carry

        lax.fori_loop(0, tiles // 2, body, 0, unroll=8)

    for copy in local[4:]:
        copy.wait()
    imp_copy.wait_recv()
    pg_arrived(0, 1)
    spread_slab(z)
    arrived(0, 1)
    process([z])
    for d in range(1, half):
        for step in (d, -d):
            for dy in range(2):
                if d != 2:
                    pg_arrived(step, dy)
            spread_slab(plane(step))
        for step in (d, -d):
            for dy in range(2):
                if d != 2:
                    arrived(step, dy)
        process([plane(d), plane(-d)])
    for dy in range(2):
        pg_arrived(half, dy)
    spread_slab(plane(half))
    for dy in range(2):
        arrived(half, dy)
    process([plane(half)])

    price_rows = []
    goal_rows = []
    for r in range(packed):
        even = pg[2 * r]
        odd = pg[2 * r + 1]
        price_rows.append(jnp.where(low, even, pltpu.roll(odd, width, 1)))
        goal_rows.append(jnp.where(low, pltpu.roll(even, width, 1), odd))
    price = jnp.concatenate(price_rows, axis=0)
    goal = jnp.concatenate(goal_rows, axis=0)

    v_lane = jnp.exp(price)

    def exchange_norms(phase):
        lse[phase, me_x] = mx_row[...] + jnp.log(zt_row[...])
        copies = []
        for k in far_first:
            copy = pltpu.make_async_remote_copy(
                src_ref=lse.at[phase, me_x],
                dst_ref=lse.at[phase, me_x],
                send_sem=x_send.at[phase, k],
                recv_sem=x_recv.at[phase, me_x],
                device_id=cre_peer(k),
                device_id_type=MESH,
            )
            copy.start()
            copies.append(copy)
        for k in range(1, n_x):
            other = lax.rem(me_x + k, n_x)
            pltpu.make_async_remote_copy(
                src_ref=lse.at[phase, me_x],
                dst_ref=lse.at[phase, other],
                send_sem=x_send.at[phase, k],
                recv_sem=x_recv.at[phase, other],
                device_id=cre_peer(k),
                device_id_type=MESH,
            ).wait_recv()
        most = lse[phase, 0]
        for k in range(1, n_x):
            most = jnp.maximum(most, lse[phase, k])
        total = jnp.exp(lse[phase, 0] - most)
        for k in range(1, n_x):
            total = total + jnp.exp(lse[phase, k] - most)
        norm = most + jnp.log(total)
        norms[0] = norm[:own_tiles]
        norms[1] = norm[own_tiles:]
        weight = jnp.concatenate([wl[0, :own_tiles], wl[1, :own_tiles]], axis=0)
        gain = weight * jnp.exp(mx_row[...] - norm)
        for t in range(tiles):
            grow[t] = jnp.broadcast_to(gain[t : t + 1, :], (8, TILE))
        return copies

    def spends():
        ones = []
        for r in range(packed):

            def body(t, acc):
                gain = grow[t]
                out = []
                for h in range(2):
                    first = r * TILE + h * width
                    k = kmat[t, first : first + width, :].reshape(width // 8, 8, TILE)
                    out.append(acc[h] + k * (factor[t, 2 * r + h] * gain))
                return tuple(out)

            zero = jnp.zeros((width // 8, 8, TILE), F32)
            a0, a1 = lax.fori_loop(0, tiles, body, (zero, zero), unroll=4)
            both = jnp.concatenate([a0, a1], axis=0).reshape(TILE, TILE)
            ones.append(jnp.sum(jnp.transpose(both), axis=0, keepdims=True))
        return ones

    for t in range(tiles):
        lim = top[t]
        m = jnp.max(jnp.max(lim, axis=0), axis=0, keepdims=True)
        mx_row[t : t + 1, :] = m
        f = jnp.exp(lim - m)
        factor[t] = f
        zt_row[t : t + 1, :] = jnp.sum(jnp.sum(f * zsum[t], axis=0), axis=0, keepdims=True)
    x_copies = exchange_norms(0)

    part1[q] = jnp.concatenate(spends(), axis=0) * v_lane
    y_copies = []
    for k in range(n_chip - 1):
        copy = pltpu.make_async_remote_copy(
            src_ref=part1.at[q],
            dst_ref=part1.at[q],
            send_sem=y_send.at[0, k],
            recv_sem=y_recv.at[0, q],
            device_id=at(*chips[k]),
            device_id_type=MESH,
        )
        copy.start()
        y_copies.append(copy)
    for k in range(n_chip - 1):
        other = slot_of(*chips[k])
        pltpu.make_async_remote_copy(
            src_ref=part1.at[q],
            dst_ref=part1.at[other],
            send_sem=y_send.at[0, k],
            recv_sem=y_recv.at[0, other],
            device_id=at(*chips[k]),
            device_id_type=MESH,
        ).wait_recv()
    spend = part1[0]
    for k in range(1, n_chip):
        spend = spend + part1[k]
    price = price + STEP_RATE * (jnp.log(goal) - jnp.log(spend + 0.25 * goal))
    v_lane = spread(price)

    group = 4

    def zbody(n, carry):
        acc = [jnp.zeros((8, TILE), F32)] * group
        for b in range(n_chip):
            place = slice(b * width, (b + 1) * width)
            v = vcol[place, :].reshape(width // 8, 8, TILE)
            for m in range(group):
                t = n * group + m
                part = jnp.sum(kmat[t, place, :].reshape(width // 8, 8, TILE) * v, axis=0)
                acc[m] = acc[m] + part * factor[t, b]
        for m in range(group):
            zt_row[pl.ds(n * group + m, 1), :] = jnp.sum(acc[m], axis=0, keepdims=True)
        return carry

    lax.fori_loop(0, tiles // group, zbody, 0)
    x_copies += exchange_norms(1)

    for r, value in enumerate(spends()):
        part2[r] = value * v_lane[r : r + 1, :]
    for k in range(n_chip - 1):
        other, peer = slot_of(*chips[k]), at(*chips[k])
        copy = pltpu.make_async_remote_copy(
            src_ref=part2.at[other // 2],
            dst_ref=got2.at[q],
            send_sem=y_send.at[1, k],
            recv_sem=y_recv.at[1, q],
            device_id=peer,
            device_id_type=MESH,
        )
        copy.start()
        y_copies.append(copy)
    got2[q] = part2[q // 2]
    norm_ref[...] = norms[c]
    for k in range(n_chip - 1):
        other = slot_of(*chips[k])
        pltpu.make_async_remote_copy(
            src_ref=part2.at[0],
            dst_ref=got2.at[other],
            send_sem=y_send.at[1, k],
            recv_sem=y_recv.at[1, other],
            device_id=at(*chips[k]),
            device_id_type=MESH,
        ).wait_recv()
    spend = got2[0]
    for k in range(1, n_chip // 2):
        spend = spend + got2[k]
    spend_b = got2[n_chip // 2]
    for k in range(n_chip // 2 + 1, n_chip):
        spend_b = spend_b + got2[k]

    row = lax.broadcasted_iota(jnp.int32, (packed, TILE), 0)

    def own_half(value):
        return jnp.where(y == 0, value, pltpu.roll(value, width, 1))[:, :width]

    price_row = jnp.sum(jnp.where(row == z, price, 0.0), axis=0, keepdims=True)
    spend_ref[0:1] = own_half(spend)
    spend_ref[1:2] = own_half(spend_b)
    spend_ref[2:3] = own_half(price_row)

    for copy in sent + core_copies + pg_copies + x_copies + y_copies:
        copy.wait_send()


def solution(mesh):
    n_chip = mesh.shape["imp"] // 2
    n_cre = mesh.shape["cre"]
    half = n_chip // 4

    def step(impressions, panels, block_lists, block_counts, imp_weight, spend_goals, prices):
        rows, wide = impressions.shape
        width = panels.shape[1]
        own_tiles = rows // TILE
        tiles = 2 * own_tiles
        n_x = n_cre * 2
        creatives = n_chip * width
        any_spec = pl.BlockSpec(memory_space=pl.ANY)
        vmem = pl.BlockSpec(memory_space=pltpu.VMEM)
        dma = pltpu.SemaphoreType.DMA
        tail, norms = pl.pallas_call(
            functools.partial(kernel, n_chip, n_cre),
            out_shape=(
                jax.ShapeDtypeStruct((3, width), F32),
                jax.ShapeDtypeStruct((own_tiles, TILE), F32),
            ),
            in_specs=[
                any_spec,
                any_spec,
                any_spec,
                pl.BlockSpec(memory_space=pltpu.SMEM),
                any_spec,
                any_spec,
                any_spec,
            ],
            out_specs=(vmem, vmem),
            scratch_shapes=[
                pltpu.VMEM((2 * rows, wide), jnp.bfloat16),
                pltpu.VMEM((creatives, wide), jnp.bfloat16),
                pltpu.VMEM((tiles, creatives, TILE), F32),
                pltpu.VMEM((tiles, n_chip, 8, TILE), F32),
                pltpu.VMEM((tiles, n_chip, 8, TILE), F32),
                pltpu.VMEM((tiles, n_chip, 8, TILE), F32),
                pltpu.VMEM((tiles, n_chip, 8, TILE), F32),
                pltpu.VMEM((tiles, 8, TILE), F32),
                pltpu.VMEM((creatives, TILE), F32),
                pltpu.VMEM((2, tiles, TILE), F32),
                pltpu.VMEM((own_tiles, block_lists.shape[1]), jnp.int32),
                pltpu.VMEM((2, 1, width), F32),
                pltpu.VMEM((n_chip, 1, TILE), F32),
                pltpu.VMEM((tiles, TILE), F32),
                pltpu.VMEM((tiles, TILE), F32),
                pltpu.VMEM((2, n_x, tiles, TILE), F32),
                pltpu.VMEM((2, own_tiles, TILE), F32),
                pltpu.VMEM((n_chip, n_chip // 2, TILE), F32),
                pltpu.VMEM((n_chip // 2, 1, TILE), F32),
                pltpu.VMEM((n_chip, 1, TILE), F32),
                dma((6,)),
                dma((n_chip - 1,)),
                dma((n_chip,)),
                dma((n_chip,)),
                dma((n_chip,)),
                dma((2,)),
                dma((2,)),
                dma((2, n_x)),
                dma((2, n_x)),
                dma((2, n_chip)),
                dma((2, n_chip)),
            ],
            compiler_params=pltpu.CompilerParams(
                collective_id=0, has_side_effects=True, vmem_limit_bytes=63 << 20
            ),
        )(
            impressions,
            panels.reshape(width, wide),
            block_lists,
            block_counts,
            imp_weight.reshape(own_tiles, TILE),
            spend_goals,
            prices,
        )
        spend = tail[0:1] + tail[1:2]
        change = jnp.log(spend_goals) - jnp.log(spend + 0.25 * spend_goals)
        return tail[2:3] + STEP_RATE * change, spend, norms.reshape(rows)

    return jax.shard_map(
        step,
        mesh=mesh,
        in_specs=(
            P("imp", None),
            P("cre", "imp", None),
            P("imp", None),
            P("imp"),
            P("imp"),
            P("cre", "imp"),
            P("cre", "imp"),
        ),
        out_specs=(P("cre", "imp"), P("cre", "imp"), P("imp")),
        check_vma=False,
    )
```

```python
import functools
import math

import jax
import jax.numpy as jnp
from jax import lax
from jax.experimental import pallas as pl
from jax.experimental.pallas import tpu as pltpu
from jax.sharding import PartitionSpec as P

MESH = pl.DeviceIdType.MESH
F32 = jnp.float32
TILE = 128
NEG_FILL = -1e30
TAU_INV = 4.0
STEP_RATE = 0.5
EXP2_SCALE = TAU_INV * math.log2(math.e)


def kernel(
    n_chip,
    n_cre,
    imp_hbm,
    panel_hbm,
    list_hbm,
    count_ref,
    weight_hbm,
    goal_hbm,
    price_hbm,
    spend_ref,
    norm_ref,
    imps,
    panels,
    kmat,
    top,
    zsum,
    bias,
    factor,
    grow,
    vcol,
    wl,
    lists,
    pg_own,
    pg,
    mx_row,
    zt_row,
    lse,
    norms,
    part1,
    part2,
    got2,
    whole,
    local_sem,
    panel_send,
    panel_recv,
    pg_send,
    pg_recv,
    core_send,
    core_recv,
    x_send,
    x_recv,
    y_send,
    y_recv,
):
    i = lax.axis_index("imp")
    g = lax.axis_index("cre")
    c = lax.rem(i, 2)
    q = i // 2
    y = lax.rem(q, 2)
    z = q // 2
    nz = n_chip // 2
    half = nz // 2
    n_x = n_cre * 2
    me_x = g * 2 + c
    rows = imp_hbm.shape[0]
    width = panel_hbm.shape[0]
    tiles = 2 * rows // TILE
    own_tiles = tiles // 2
    packed = n_chip // 2

    mirror = g + 1 - 2 * lax.rem(g, 2)

    def plane(step):
        return lax.rem(z + step + nz, nz)

    def slot_of(step, dy):
        return plane(step) * 2 + (y if dy == 0 else 1 - y)

    def rel(step, dy):
        return step % nz * 2 + dy

    def at(step, dy):
        return {"imp": slot_of(step, dy) * 2 + c, "cre": g if dy == 0 else mirror}

    chips = [(half, 1), (half, 0)]
    for d in range(half - 1, 0, -1):
        chips += [(d, 1), (-d, 1), (d, 0), (-d, 0)]
    chips += [(0, 1)]

    def cre_peer(k):
        other = lax.rem(me_x + k, n_x)
        return {"imp": q * 2 + lax.rem(other, 2), "cre": other // 2}

    far_first = sorted(range(1, n_x), key=lambda k: -min(k, n_x - k))
    core_peer = {"imp": q * 2 + 1 - c, "cre": g}

    barrier = pltpu.get_barrier_semaphore()
    near = [(step, dy) for step, dy in chips if abs(step) <= 2]
    for step, dy in near:
        pl.semaphore_signal(barrier, inc=1, device_id=at(step, dy), device_id_type=MESH)
    for k in far_first:
        pl.semaphore_signal(barrier, inc=1, device_id=cre_peer(k), device_id_type=MESH)

    own_rows = pl.ds(pl.multiple_of(c * rows, rows), rows)

    def shard_ref(slot):
        return panels.at[pl.ds(slot * width, width)]

    local = [
        pltpu.make_async_copy(price_hbm, pg_own.at[0], local_sem.at[0]),
        pltpu.make_async_copy(goal_hbm, pg_own.at[1], local_sem.at[1]),
        pltpu.make_async_copy(list_hbm, lists, local_sem.at[2]),
        pltpu.make_async_copy(weight_hbm, wl.at[c, pl.ds(0, own_tiles)], local_sem.at[3]),
        pltpu.make_async_copy(panel_hbm, shard_ref(0), local_sem.at[4]),
        pltpu.make_async_copy(imp_hbm, imps.at[own_rows], local_sem.at[5]),
    ]
    for copy in local:
        copy.start()

    for copy in local[:2]:
        copy.wait()
    pg[0] = jnp.concatenate([pg_own[0], pg_own[1]], axis=1)
    pl.semaphore_wait(barrier, len(near) + n_x - 1)

    pg_copies = []

    def pg_copy(src, dst, peer, n=0):
        return pltpu.make_async_remote_copy(
            src_ref=pg.at[src],
            dst_ref=pg.at[dst],
            send_sem=pg_send.at[n],
            recv_sem=pg_recv.at[dst],
            device_id=peer,
            device_id_type=MESH,
        )

    def pg_put(src, dst, peer):
        copy = pg_copy(src, dst, peer, len(pg_copies))
        copy.start()
        pg_copies.append(copy)

    def pg_arrived(step, dy):
        pg_copy(0, rel(step, dy), at(0, 1)).wait_recv()

    for step, dy in near:
        pg_put(0, rel(-step, dy), at(step, dy))

    sent = []

    def panel_copy(src, slot, peer, n=0):
        return pltpu.make_async_remote_copy(
            src_ref=src,
            dst_ref=shard_ref(slot),
            send_sem=panel_send.at[n],
            recv_sem=panel_recv.at[slot],
            device_id=peer,
            device_id_type=MESH,
        )

    def send(src, slot, peer):
        copy = panel_copy(src, slot, peer, len(sent))
        copy.start()
        sent.append(copy)

    def arrived(step, dy):
        panel_copy(panel_hbm, rel(step, dy), at(0, 1)).wait_recv()

    for step in (2, -2, 1, -1):
        for dy in (1, 0):
            send(panel_hbm, rel(-step, dy), at(step, dy))
    send(panel_hbm, rel(0, 1), at(0, 1))

    imp_copy = pltpu.make_async_remote_copy(
        src_ref=imp_hbm,
        dst_ref=imps.at[own_rows],
        send_sem=core_send.at[1],
        recv_sem=core_recv.at[1],
        device_id=core_peer,
        device_id_type=MESH,
    )
    imp_copy.start()

    for copy in local[2:4]:
        copy.wait()
    sub = lax.broadcasted_iota(jnp.int32, lists.shape, 0)
    lane = lax.broadcasted_iota(jnp.int32, lists.shape, 1)
    counts = jnp.zeros(lists.shape, jnp.int32)
    for t in range(own_tiles):
        counts = jnp.where(sub == t, count_ref[t], counts)
    wl[c, pl.ds(own_tiles, own_tiles)] = jnp.full((own_tiles, TILE), -1.0, F32)
    wl[c, pl.ds(own_tiles, own_tiles), pl.ds(0, lists.shape[1])] = jnp.where(
        lane < counts, lists[...].astype(F32), -1.0
    )
    wl_copy = pltpu.make_async_remote_copy(
        src_ref=wl.at[c],
        dst_ref=wl.at[c],
        send_sem=core_send.at[0],
        recv_sem=core_recv.at[0],
        device_id=core_peer,
        device_id_type=MESH,
    )
    wl_copy.start()
    core_copies = [wl_copy, imp_copy]

    wl_copy.wait_recv()
    ids = lax.broadcasted_iota(jnp.int32, (n_chip, TILE), 0)
    same = lax.rem(ids, 2) == 0
    ids = lax.rem(lax.div(ids, 2) + z, nz) * 2
    ids = ids + jnp.where(same, g * n_chip + y, mirror * n_chip + 1 - y)
    ids = ids.astype(F32)
    for t in range(tiles):
        row = wl[t // own_tiles, own_tiles + t % own_tiles : own_tiles + t % own_tiles + 1, :]
        hit = jnp.max(jnp.where(row == ids, 1.0, 0.0), axis=1, keepdims=True)
        level = jnp.broadcast_to(jnp.where(hit > 0.0, 0.0, NEG_FILL), (n_chip, TILE))
        for b in range(n_chip):
            bias[t, b] = jnp.broadcast_to(level[b : b + 1, :], (8, TILE))

    for sign in (1, -1):
        for s in range(2):
            dy = s if sign == 1 else 1 - s
            slot = rel(-2 * sign, dy)
            pg_arrived(-2 * sign, dy)
            if s == 0:
                pg_put(slot, rel(half, dy), at(2 * sign, 0))
            pg_put(slot, rel(-3 * sign, dy), at(sign, 0))
            arrived(-2 * sign, dy)
            if s == 0:
                send(shard_ref(slot), rel(half, dy), at(2 * sign, 0))
            send(shard_ref(slot), rel(-3 * sign, dy), at(sign, 0))

    low = lax.broadcasted_iota(jnp.int32, (1, TILE), 1) < width
    def spread_row(d, row):
        v = jnp.exp(row)
        vcol[d * TILE : (d + 1) * TILE, :] = jnp.transpose(jnp.broadcast_to(v, (TILE, TILE)))
        return v

    def turned(row):
        return jnp.where(y == 0, row, pltpu.roll(row, width, 1))

    def plane_row(d):
        return pl.ds(plane(d), 1)

    values = {}

    def spread_slab(step):
        d = step % nz
        even, odd = pg[2 * d], pg[2 * d + 1]
        row = jnp.where(low, even, pltpu.roll(odd, width, 1))
        values[d] = spread_row(d, row)
        whole[0, plane_row(d), :] = turned(row)
        whole[1, plane_row(d), :] = turned(jnp.where(low, pltpu.roll(even, width, 1), odd))

    slab_rows = 2 * width

    def process(slabs):
        parts = []
        for zz in slabs:
            parts.append(panels[zz * slab_rows : (zz + 1) * slab_rows, :])
        pan = parts[0] if len(parts) == 1 else jnp.concatenate(parts, axis=0)

        def body(t2, carry):
            x = imps[pl.ds(pl.multiple_of(t2 * 2 * TILE, 2 * TILE), 2 * TILE), :]
            aff = lax.dot_general(pan, x, (((1,), (1,)), ((), ())), preferred_element_type=F32)
            for n, zz in enumerate(slabs):
                for h in range(2):
                    qq = zz * 2 + h
                    place = slice(qq * width, (qq + 1) * width)
                    v = vcol[place, :].reshape(width // 8, 8, TILE)
                    for side in range(2):
                        t = t2 * 2 + side
                        first = n * slab_rows + h * width
                        a = aff[first : first + width, side * TILE : (side + 1) * TILE]
                        a = a.reshape(width // 8, 8, TILE)
                        m = jnp.max(a, axis=0)
                        e = jnp.exp2((a - m) * EXP2_SCALE)
                        kmat[t, place, :] = e.reshape(width, TILE)
                        top[t, qq] = TAU_INV * m + bias[t, qq]
                        zsum[t, qq] = jnp.sum(e * v, axis=0)
            return carry

        lax.fori_loop(0, tiles // 2, body, 0, unroll=8)

    for copy in local[4:]:
        copy.wait()
    imp_copy.wait_recv()
    pg_arrived(0, 1)
    spread_slab(0)
    arrived(0, 1)
    process([0])
    for d in range(1, half):
        for step in (d, -d):
            for dy in range(2):
                if d != 2:
                    pg_arrived(step, dy)
            spread_slab(step)
        for step in (d, -d):
            for dy in range(2):
                if d != 2:
                    arrived(step, dy)
        process([d, nz - d])
    for dy in range(2):
        pg_arrived(half, dy)
    spread_slab(half)
    for dy in range(2):
        arrived(half, dy)
    process([half])

    def exchange_norms(phase):
        lse[phase, me_x] = mx_row[...] + jnp.log(zt_row[...])
        copies = []
        for k in far_first:
            copy = pltpu.make_async_remote_copy(
                src_ref=lse.at[phase, me_x],
                dst_ref=lse.at[phase, me_x],
                send_sem=x_send.at[phase, k],
                recv_sem=x_recv.at[phase, me_x],
                device_id=cre_peer(k),
                device_id_type=MESH,
            )
            copy.start()
            copies.append(copy)
        for k in range(1, n_x):
            other = lax.rem(me_x + k, n_x)
            pltpu.make_async_remote_copy(
                src_ref=lse.at[phase, me_x],
                dst_ref=lse.at[phase, other],
                send_sem=x_send.at[phase, k],
                recv_sem=x_recv.at[phase, other],
                device_id=cre_peer(k),
                device_id_type=MESH,
            ).wait_recv()
        most = lse[phase, 0]
        for k in range(1, n_x):
            most = jnp.maximum(most, lse[phase, k])
        total = jnp.exp(lse[phase, 0] - most)
        for k in range(1, n_x):
            total = total + jnp.exp(lse[phase, k] - most)
        norm = most + jnp.log(total)
        norms[0] = norm[:own_tiles]
        norms[1] = norm[own_tiles:]
        weight = jnp.concatenate([wl[0, :own_tiles], wl[1, :own_tiles]], axis=0)
        gain = weight * jnp.exp(mx_row[...] - norm)
        for t in range(tiles):
            grow[t] = jnp.broadcast_to(gain[t : t + 1, :], (8, TILE))
        return copies

    def spends():
        ones = []
        for r in range(packed):

            def body(t, acc):
                gain = grow[t]
                out = []
                for h in range(2):
                    first = r * TILE + h * width
                    k = kmat[t, first : first + width, :].reshape(width // 8, 8, TILE)
                    out.append(acc[h] + k * (factor[t, 2 * r + h] * gain))
                return tuple(out)

            zero = jnp.zeros((width // 8, 8, TILE), F32)
            a0, a1 = lax.fori_loop(0, tiles, body, (zero, zero), unroll=tiles)
            both = jnp.concatenate([a0, a1], axis=0).reshape(TILE, TILE)
            ones.append(jnp.sum(jnp.transpose(both), axis=0, keepdims=True))
        return ones

    for t in range(tiles):
        lim = top[t]
        m = jnp.max(jnp.max(lim, axis=0), axis=0, keepdims=True)
        mx_row[t : t + 1, :] = m
        f = jnp.exp(lim - m)
        factor[t] = f
        zt_row[t : t + 1, :] = jnp.sum(jnp.sum(f * zsum[t], axis=0), axis=0, keepdims=True)
    x_copies = exchange_norms(0)

    for d, value in enumerate(spends()):
        part1[q, plane_row(d), :] = turned(value * values[d])
    y_copies = []
    for k in range(n_chip - 1):
        copy = pltpu.make_async_remote_copy(
            src_ref=part1.at[q],
            dst_ref=part1.at[q],
            send_sem=y_send.at[0, k],
            recv_sem=y_recv.at[0, q],
            device_id=at(*chips[k]),
            device_id_type=MESH,
        )
        copy.start()
        y_copies.append(copy)
    for k in range(n_chip - 1):
        other = slot_of(*chips[k])
        pltpu.make_async_remote_copy(
            src_ref=part1.at[q],
            dst_ref=part1.at[other],
            send_sem=y_send.at[0, k],
            recv_sem=y_recv.at[0, other],
            device_id=at(*chips[k]),
            device_id_type=MESH,
        ).wait_recv()
    spend = part1[0]
    for k in range(1, n_chip):
        spend = spend + part1[k]
    goal = whole[1]
    whole[0] = whole[0] + STEP_RATE * (jnp.log(goal) - jnp.log(spend + 0.25 * goal))
    for d in range(nz):
        row = turned(whole[0, plane_row(d), :])
        values[d] = spread_row(d, row)
        if d == 0:
            price_row = row

    group = 4

    def zbody(n, carry):
        acc = [jnp.zeros((8, TILE), F32)] * group
        for b in range(n_chip):
            place = slice(b * width, (b + 1) * width)
            v = vcol[place, :].reshape(width // 8, 8, TILE)
            for m in range(group):
                t = n * group + m
                part = jnp.sum(kmat[t, place, :].reshape(width // 8, 8, TILE) * v, axis=0)
                acc[m] = acc[m] + part * factor[t, b]
        for m in range(group):
            zt_row[pl.ds(n * group + m, 1), :] = jnp.sum(acc[m], axis=0, keepdims=True)
        return carry

    lax.fori_loop(0, tiles // group, zbody, 0)
    x_copies += exchange_norms(1)

    for d, value in enumerate(spends()):
        part2[d] = value * values[d]

    def row_copy(step, dy, n):
        return pltpu.make_async_remote_copy(
            src_ref=part2.at[step % nz],
            dst_ref=got2.at[rel(-step, dy)],
            send_sem=y_send.at[1, n],
            recv_sem=y_recv.at[1, rel(-step, dy)],
            device_id=at(step, dy),
            device_id_type=MESH,
        )

    for n, (step, dy) in enumerate(chips):
        copy = row_copy(step, dy, n)
        copy.start()
        y_copies.append(copy)
    got2[0] = part2[0]
    norm_ref[...] = norms[c]
    for step, dy in chips:
        row_copy(-step, dy, 0).wait_recv()
    sums = []
    for dy in range(2):
        total = got2[dy]
        for d in range(1, nz):
            total = total + got2[2 * d + dy]
        sums.append(total)
    spend_ref[0:1] = sums[0][:, :width]
    spend_ref[1:2] = pltpu.roll(sums[1], width, 1)[:, :width]
    spend_ref[2:3] = price_row[:, :width]

    for copy in sent + core_copies + pg_copies + x_copies + y_copies:
        copy.wait_send()


def solution(mesh):
    n_chip = mesh.shape["imp"] // 2
    n_cre = mesh.shape["cre"]
    half = n_chip // 4

    def step(impressions, panels, block_lists, block_counts, imp_weight, spend_goals, prices):
        rows, wide = impressions.shape
        width = panels.shape[1]
        own_tiles = rows // TILE
        tiles = 2 * own_tiles
        n_x = n_cre * 2
        creatives = n_chip * width
        any_spec = pl.BlockSpec(memory_space=pl.ANY)
        vmem = pl.BlockSpec(memory_space=pltpu.VMEM)
        dma = pltpu.SemaphoreType.DMA
        tail, norms = pl.pallas_call(
            functools.partial(kernel, n_chip, n_cre),
            out_shape=(
                jax.ShapeDtypeStruct((3, width), F32),
                jax.ShapeDtypeStruct((own_tiles, TILE), F32),
            ),
            in_specs=[
                any_spec,
                any_spec,
                any_spec,
                pl.BlockSpec(memory_space=pltpu.SMEM),
                any_spec,
                any_spec,
                any_spec,
            ],
            out_specs=(vmem, vmem),
            scratch_shapes=[
                pltpu.VMEM((2 * rows, wide), jnp.bfloat16),
                pltpu.VMEM((creatives, wide), jnp.bfloat16),
                pltpu.VMEM((tiles, creatives, TILE), F32),
                pltpu.VMEM((tiles, n_chip, 8, TILE), F32),
                pltpu.VMEM((tiles, n_chip, 8, TILE), F32),
                pltpu.VMEM((tiles, n_chip, 8, TILE), F32),
                pltpu.VMEM((tiles, n_chip, 8, TILE), F32),
                pltpu.VMEM((tiles, 8, TILE), F32),
                pltpu.VMEM((creatives, TILE), F32),
                pltpu.VMEM((2, tiles, TILE), F32),
                pltpu.VMEM((own_tiles, block_lists.shape[1]), jnp.int32),
                pltpu.VMEM((2, 1, width), F32),
                pltpu.VMEM((n_chip, 1, TILE), F32),
                pltpu.VMEM((tiles, TILE), F32),
                pltpu.VMEM((tiles, TILE), F32),
                pltpu.VMEM((2, n_x, tiles, TILE), F32),
                pltpu.VMEM((2, own_tiles, TILE), F32),
                pltpu.VMEM((n_chip, n_chip // 2, TILE), F32),
                pltpu.VMEM((n_chip // 2, 1, TILE), F32),
                pltpu.VMEM((n_chip, 1, TILE), F32),
                pltpu.VMEM((2, n_chip // 2, TILE), F32),
                dma((6,)),
                dma((n_chip - 1,)),
                dma((n_chip,)),
                dma((n_chip,)),
                dma((n_chip,)),
                dma((2,)),
                dma((2,)),
                dma((2, n_x)),
                dma((2, n_x)),
                dma((2, n_chip)),
                dma((2, n_chip)),
            ],
            compiler_params=pltpu.CompilerParams(
                collective_id=0, has_side_effects=True, vmem_limit_bytes=63 << 20
            ),
        )(
            impressions,
            panels.reshape(width, wide),
            block_lists,
            block_counts,
            imp_weight.reshape(own_tiles, TILE),
            spend_goals,
            prices,
        )
        spend = tail[0:1] + tail[1:2]
        change = jnp.log(spend_goals) - jnp.log(spend + 0.25 * spend_goals)
        return tail[2:3] + STEP_RATE * change, spend, norms.reshape(rows)

    return jax.shard_map(
        step,
        mesh=mesh,
        in_specs=(
            P("imp", None),
            P("cre", "imp", None),
            P("imp", None),
            P("imp"),
            P("imp"),
            P("cre", "imp"),
            P("cre", "imp"),
        ),
        out_specs=(P("cre", "imp"), P("cre", "imp"), P("imp")),
        check_vma=False,
    )
```

```python
import functools
import math

import jax
import jax.numpy as jnp
from jax import lax
from jax.experimental import pallas as pl
from jax.experimental.pallas import tpu as pltpu
from jax.sharding import PartitionSpec as P

MESH = pl.DeviceIdType.MESH
F32 = jnp.float32
TILE = 128
NEG_FILL = -1e30
TAU_INV = 4.0
STEP_RATE = 0.5
EXP2_SCALE = TAU_INV * math.log2(math.e)


def kernel(
    n_chip,
    n_cre,
    imp_hbm,
    panel_hbm,
    list_hbm,
    count_ref,
    weight_hbm,
    goal_hbm,
    price_hbm,
    new_price_ref,
    spend_ref,
    norm_ref,
    imps,
    panels,
    kmat,
    top,
    zsum,
    bias,
    factor,
    grow,
    vcol,
    wl,
    lists,
    pg_own,
    pg,
    mx_row,
    zt_row,
    lse,
    norms,
    part1,
    part2,
    got2,
    whole,
    local_sem,
    panel_send,
    panel_recv,
    pg_send,
    pg_recv,
    core_send,
    core_recv,
    x_send,
    x_recv,
    y_send,
    y_recv,
):
    i = lax.axis_index("imp")
    g = lax.axis_index("cre")
    c = lax.rem(i, 2)
    q = i // 2
    y = lax.rem(q, 2)
    z = q // 2
    nz = n_chip // 2
    half = nz // 2
    n_x = n_cre * 2
    me_x = g * 2 + c
    rows = imp_hbm.shape[0]
    width = panel_hbm.shape[0]
    tiles = 2 * rows // TILE
    own_tiles = tiles // 2
    packed = n_chip // 2

    mirror = g + 1 - 2 * lax.rem(g, 2)

    def plane(step):
        return lax.rem(z + step + nz, nz)

    def slot_of(step, dy):
        return plane(step) * 2 + (y if dy == 0 else 1 - y)

    def rel(step, dy):
        return step % nz * 2 + dy

    def at(step, dy):
        return {"imp": slot_of(step, dy) * 2 + c, "cre": g if dy == 0 else mirror}

    chips = [(half, 1), (half, 0)]
    for d in range(half - 1, 0, -1):
        chips += [(d, 1), (-d, 1), (d, 0), (-d, 0)]
    chips += [(0, 1)]

    def cre_peer(k):
        other = lax.rem(me_x + k, n_x)
        return {"imp": q * 2 + lax.rem(other, 2), "cre": other // 2}

    far_first = sorted(range(1, n_x), key=lambda k: -min(k, n_x - k))
    core_peer = {"imp": q * 2 + 1 - c, "cre": g}

    barrier = pltpu.get_barrier_semaphore()
    near = [(step, dy) for step, dy in chips if abs(step) <= 2]
    for step, dy in near:
        pl.semaphore_signal(barrier, inc=1, device_id=at(step, dy), device_id_type=MESH)
    for k in far_first:
        pl.semaphore_signal(barrier, inc=1, device_id=cre_peer(k), device_id_type=MESH)

    own_rows = pl.ds(pl.multiple_of(c * rows, rows), rows)

    def shard_ref(slot):
        return panels.at[pl.ds(slot * width, width)]

    local = [
        pltpu.make_async_copy(price_hbm, pg_own.at[0], local_sem.at[0]),
        pltpu.make_async_copy(goal_hbm, pg_own.at[1], local_sem.at[1]),
        pltpu.make_async_copy(list_hbm, lists, local_sem.at[2]),
        pltpu.make_async_copy(weight_hbm, wl.at[c, pl.ds(0, own_tiles)], local_sem.at[3]),
        pltpu.make_async_copy(panel_hbm, shard_ref(0), local_sem.at[4]),
        pltpu.make_async_copy(imp_hbm, imps.at[own_rows], local_sem.at[5]),
    ]
    for copy in local:
        copy.start()

    for copy in local[:2]:
        copy.wait()
    pg[0] = jnp.concatenate([pg_own[0], pg_own[1]], axis=1)
    pl.semaphore_wait(barrier, len(near) + n_x - 1)

    pg_copies = []

    def pg_copy(src, dst, peer, n=0):
        return pltpu.make_async_remote_copy(
            src_ref=pg.at[src],
            dst_ref=pg.at[dst],
            send_sem=pg_send.at[n],
            recv_sem=pg_recv.at[dst],
            device_id=peer,
            device_id_type=MESH,
        )

    def pg_put(src, dst, peer):
        copy = pg_copy(src, dst, peer, len(pg_copies))
        copy.start()
        pg_copies.append(copy)

    def pg_arrived(step, dy):
        pg_copy(0, rel(step, dy), at(0, 1)).wait_recv()

    for step, dy in near:
        pg_put(0, rel(-step, dy), at(step, dy))

    sent = []

    def panel_copy(src, slot, peer, n=0):
        return pltpu.make_async_remote_copy(
            src_ref=src,
            dst_ref=shard_ref(slot),
            send_sem=panel_send.at[n],
            recv_sem=panel_recv.at[slot],
            device_id=peer,
            device_id_type=MESH,
        )

    def send(src, slot, peer):
        copy = panel_copy(src, slot, peer, len(sent))
        copy.start()
        sent.append(copy)

    def arrived(step, dy):
        panel_copy(panel_hbm, rel(step, dy), at(0, 1)).wait_recv()

    for step in (2, -2, 1, -1):
        for dy in (1, 0):
            send(panel_hbm, rel(-step, dy), at(step, dy))
    send(panel_hbm, rel(0, 1), at(0, 1))

    imp_copy = pltpu.make_async_remote_copy(
        src_ref=imp_hbm,
        dst_ref=imps.at[own_rows],
        send_sem=core_send.at[1],
        recv_sem=core_recv.at[1],
        device_id=core_peer,
        device_id_type=MESH,
    )
    imp_copy.start()

    for copy in local[2:4]:
        copy.wait()
    sub = lax.broadcasted_iota(jnp.int32, lists.shape, 0)
    lane = lax.broadcasted_iota(jnp.int32, lists.shape, 1)
    counts = jnp.zeros(lists.shape, jnp.int32)
    for t in range(own_tiles):
        counts = jnp.where(sub == t, count_ref[t], counts)
    wl[c, pl.ds(own_tiles, own_tiles)] = jnp.full((own_tiles, TILE), -1.0, F32)
    wl[c, pl.ds(own_tiles, own_tiles), pl.ds(0, lists.shape[1])] = jnp.where(
        lane < counts, lists[...].astype(F32), -1.0
    )
    wl_copy = pltpu.make_async_remote_copy(
        src_ref=wl.at[c],
        dst_ref=wl.at[c],
        send_sem=core_send.at[0],
        recv_sem=core_recv.at[0],
        device_id=core_peer,
        device_id_type=MESH,
    )
    wl_copy.start()
    core_copies = [wl_copy, imp_copy]

    wl_copy.wait_recv()
    ids = lax.broadcasted_iota(jnp.int32, (n_chip, TILE), 0)
    same = lax.rem(ids, 2) == 0
    ids = lax.rem(lax.div(ids, 2) + z, nz) * 2
    ids = ids + jnp.where(same, g * n_chip + y, mirror * n_chip + 1 - y)
    ids = ids.astype(F32)
    for t in range(tiles):
        row = wl[t // own_tiles, own_tiles + t % own_tiles : own_tiles + t % own_tiles + 1, :]
        hit = jnp.max(jnp.where(row == ids, 1.0, 0.0), axis=1, keepdims=True)
        level = jnp.broadcast_to(jnp.where(hit > 0.0, 0.0, NEG_FILL), (n_chip, TILE))
        for b in range(n_chip):
            bias[t, b] = jnp.broadcast_to(level[b : b + 1, :], (8, TILE))

    for sign in (1, -1):
        for s in range(2):
            dy = s if sign == 1 else 1 - s
            slot = rel(-2 * sign, dy)
            pg_arrived(-2 * sign, dy)
            if s == 0:
                pg_put(slot, rel(half, dy), at(2 * sign, 0))
            pg_put(slot, rel(-3 * sign, dy), at(sign, 0))
            arrived(-2 * sign, dy)
            if s == 0:
                send(shard_ref(slot), rel(half, dy), at(2 * sign, 0))
            send(shard_ref(slot), rel(-3 * sign, dy), at(sign, 0))

    low = lax.broadcasted_iota(jnp.int32, (1, TILE), 1) < width
    def spread_row(d, row):
        v = jnp.exp(row)
        vcol[d * TILE : (d + 1) * TILE, :] = jnp.transpose(jnp.broadcast_to(v, (TILE, TILE)))
        return v

    def turned(row):
        return jnp.where(y == 0, row, pltpu.roll(row, width, 1))

    def plane_row(d):
        return pl.ds(plane(d), 1)

    values = {}

    def spread_slab(step):
        d = step % nz
        even, odd = pg[2 * d], pg[2 * d + 1]
        row = jnp.where(low, even, pltpu.roll(odd, width, 1))
        values[d] = spread_row(d, row)
        whole[0, plane_row(d), :] = turned(row)
        whole[1, plane_row(d), :] = turned(jnp.where(low, pltpu.roll(even, width, 1), odd))

    slab_rows = 2 * width

    def process(slabs):
        parts = []
        for zz in slabs:
            parts.append(panels[zz * slab_rows : (zz + 1) * slab_rows, :])
        pan = parts[0] if len(parts) == 1 else jnp.concatenate(parts, axis=0)

        def body(t2, carry):
            x = imps[pl.ds(pl.multiple_of(t2 * 2 * TILE, 2 * TILE), 2 * TILE), :]
            aff = lax.dot_general(pan, x, (((1,), (1,)), ((), ())), preferred_element_type=F32)
            for n, zz in enumerate(slabs):
                for h in range(2):
                    qq = zz * 2 + h
                    place = slice(qq * width, (qq + 1) * width)
                    v = vcol[place, :].reshape(width // 8, 8, TILE)
                    for side in range(2):
                        t = t2 * 2 + side
                        first = n * slab_rows + h * width
                        a = aff[first : first + width, side * TILE : (side + 1) * TILE]
                        a = a.reshape(width // 8, 8, TILE)
                        m = jnp.max(a, axis=0)
                        e = jnp.exp2((a - m) * EXP2_SCALE)
                        kmat[t, place, :] = e.reshape(width, TILE)
                        top[t, qq] = TAU_INV * m + bias[t, qq]
                        zsum[t, qq] = jnp.sum(e * v, axis=0)
            return carry

        lax.fori_loop(0, tiles // 2, body, 0, unroll=8)

    for copy in local[4:]:
        copy.wait()
    imp_copy.wait_recv()
    pg_arrived(0, 1)
    spread_slab(0)
    arrived(0, 1)
    process([0])
    for d in range(1, half):
        for step in (d, -d):
            for dy in range(2):
                if d != 2:
                    pg_arrived(step, dy)
            spread_slab(step)
        for step in (d, -d):
            for dy in range(2):
                if d != 2:
                    arrived(step, dy)
        process([d, nz - d])
    for dy in range(2):
        pg_arrived(half, dy)
    spread_slab(half)
    for dy in range(2):
        arrived(half, dy)
    process([half])

    def drain(*groups):
        for group in groups:
            for copy in group:
                copy.wait_send()

    def exchange_norms(phase, earlier):
        lse[phase, me_x] = mx_row[...] + jnp.log(zt_row[...])
        copies = []
        for k in far_first:
            copy = pltpu.make_async_remote_copy(
                src_ref=lse.at[phase, me_x],
                dst_ref=lse.at[phase, me_x],
                send_sem=x_send.at[phase, k],
                recv_sem=x_recv.at[phase, me_x],
                device_id=cre_peer(k),
                device_id_type=MESH,
            )
            copy.start()
            copies.append(copy)
        drain(*earlier)
        for k in range(1, n_x):
            other = lax.rem(me_x + k, n_x)
            pltpu.make_async_remote_copy(
                src_ref=lse.at[phase, me_x],
                dst_ref=lse.at[phase, other],
                send_sem=x_send.at[phase, k],
                recv_sem=x_recv.at[phase, other],
                device_id=cre_peer(k),
                device_id_type=MESH,
            ).wait_recv()
        most = lse[phase, 0]
        for k in range(1, n_x):
            most = jnp.maximum(most, lse[phase, k])
        total = jnp.exp(lse[phase, 0] - most)
        for k in range(1, n_x):
            total = total + jnp.exp(lse[phase, k] - most)
        norm = most + jnp.log(total)
        norms[0] = norm[:own_tiles]
        norms[1] = norm[own_tiles:]
        weight = jnp.concatenate([wl[0, :own_tiles], wl[1, :own_tiles]], axis=0)
        gain = weight * jnp.exp(mx_row[...] - norm)
        for t in range(tiles):
            grow[t] = jnp.broadcast_to(gain[t : t + 1, :], (8, TILE))
        return copies

    def spends():
        ones = []
        for r in range(packed):

            def body(t, acc):
                gain = grow[t]
                out = []
                for h in range(2):
                    first = r * TILE + h * width
                    k = kmat[t, first : first + width, :].reshape(width // 8, 8, TILE)
                    out.append(acc[h] + k * (factor[t, 2 * r + h] * gain))
                return tuple(out)

            zero = jnp.zeros((width // 8, 8, TILE), F32)
            a0, a1 = lax.fori_loop(0, tiles, body, (zero, zero), unroll=tiles)
            both = jnp.concatenate([a0, a1], axis=0).reshape(TILE, TILE)
            ones.append(jnp.sum(jnp.transpose(both), axis=0, keepdims=True))
        return ones

    for t in range(tiles):
        lim = top[t]
        m = jnp.max(jnp.max(lim, axis=0), axis=0, keepdims=True)
        mx_row[t : t + 1, :] = m
        f = jnp.exp(lim - m)
        factor[t] = f
        zt_row[t : t + 1, :] = jnp.sum(jnp.sum(f * zsum[t], axis=0), axis=0, keepdims=True)
    x_copies = exchange_norms(0, (sent, core_copies, pg_copies))

    for d, value in enumerate(spends()):
        part1[q, plane_row(d), :] = turned(value * values[d])
    y_copies = []
    for k in range(n_chip - 1):
        copy = pltpu.make_async_remote_copy(
            src_ref=part1.at[q],
            dst_ref=part1.at[q],
            send_sem=y_send.at[0, k],
            recv_sem=y_recv.at[0, q],
            device_id=at(*chips[k]),
            device_id_type=MESH,
        )
        copy.start()
        y_copies.append(copy)
    drain(x_copies)
    for k in range(n_chip - 1):
        other = slot_of(*chips[k])
        pltpu.make_async_remote_copy(
            src_ref=part1.at[q],
            dst_ref=part1.at[other],
            send_sem=y_send.at[0, k],
            recv_sem=y_recv.at[0, other],
            device_id=at(*chips[k]),
            device_id_type=MESH,
        ).wait_recv()
    spend = part1[0]
    for k in range(1, n_chip):
        spend = spend + part1[k]
    goal = whole[1]
    whole[0] = whole[0] + STEP_RATE * (jnp.log(goal) - jnp.log(spend + 0.25 * goal))
    for d in range(nz):
        row = turned(whole[0, plane_row(d), :])
        values[d] = spread_row(d, row)
        if d == 0:
            price_row = row

    group = 4

    def zbody(n, carry):
        acc = [jnp.zeros((8, TILE), F32)] * group
        for b in range(n_chip):
            place = slice(b * width, (b + 1) * width)
            v = vcol[place, :].reshape(width // 8, 8, TILE)
            for m in range(group):
                t = n * group + m
                part = jnp.sum(kmat[t, place, :].reshape(width // 8, 8, TILE) * v, axis=0)
                acc[m] = acc[m] + part * factor[t, b]
        for m in range(group):
            zt_row[pl.ds(n * group + m, 1), :] = jnp.sum(acc[m], axis=0, keepdims=True)
        return carry

    lax.fori_loop(0, tiles // group, zbody, 0)
    x_last = exchange_norms(1, (y_copies,))

    for d, value in enumerate(spends()):
        part2[d] = value * values[d]

    def row_copy(step, dy, n):
        return pltpu.make_async_remote_copy(
            src_ref=part2.at[step % nz],
            dst_ref=got2.at[rel(-step, dy)],
            send_sem=y_send.at[1, n],
            recv_sem=y_recv.at[1, rel(-step, dy)],
            device_id=at(step, dy),
            device_id_type=MESH,
        )

    y_last = []
    for n, (step, dy) in enumerate(chips):
        copy = row_copy(step, dy, n)
        copy.start()
        y_last.append(copy)
    drain(x_last)
    got2[0] = part2[0]
    norm_ref[...] = norms[c]
    for step, dy in chips:
        row_copy(-step, dy, 0).wait_recv()
    sums = []
    for dy in range(2):
        total = got2[dy]
        for d in range(1, nz):
            total = total + got2[2 * d + dy]
        sums.append(total)
    spend = (sums[0] + pltpu.roll(sums[1], width, 1))[:, :width]
    goal = pg_own[1]
    change = jnp.log(goal) - jnp.log(spend + 0.25 * goal)
    spend_ref[...] = spend
    new_price_ref[...] = price_row[:, :width] + STEP_RATE * change

    drain(y_last)


def hand_on(price_ref, spend_ref, norm_ref, price_out, spend_out, norm_out, sem):
    pairs = ((price_ref, price_out), (spend_ref, spend_out), (norm_ref, norm_out))
    copies = [pltpu.make_async_copy(a, b, sem.at[n]) for n, (a, b) in enumerate(pairs)]
    for copy in copies:
        copy.start()
    for copy in copies:
        copy.wait()


def solution(mesh):
    n_chip = mesh.shape["imp"] // 2
    n_cre = mesh.shape["cre"]
    half = n_chip // 4

    def step(impressions, panels, block_lists, block_counts, imp_weight, spend_goals, prices):
        rows, wide = impressions.shape
        width = panels.shape[1]
        own_tiles = rows // TILE
        tiles = 2 * own_tiles
        n_x = n_cre * 2
        creatives = n_chip * width
        any_spec = pl.BlockSpec(memory_space=pl.ANY)
        vmem = pl.BlockSpec(memory_space=pltpu.VMEM)
        dma = pltpu.SemaphoreType.DMA
        results = pl.pallas_call(
            functools.partial(kernel, n_chip, n_cre),
            out_shape=(
                jax.ShapeDtypeStruct((1, width), F32),
                jax.ShapeDtypeStruct((1, width), F32),
                jax.ShapeDtypeStruct((own_tiles, TILE), F32),
            ),
            in_specs=[
                any_spec,
                any_spec,
                any_spec,
                pl.BlockSpec(memory_space=pltpu.SMEM),
                any_spec,
                any_spec,
                any_spec,
            ],
            out_specs=(vmem, vmem, vmem),
            scratch_shapes=[
                pltpu.VMEM((2 * rows, wide), jnp.bfloat16),
                pltpu.VMEM((creatives, wide), jnp.bfloat16),
                pltpu.VMEM((tiles, creatives, TILE), F32),
                pltpu.VMEM((tiles, n_chip, 8, TILE), F32),
                pltpu.VMEM((tiles, n_chip, 8, TILE), F32),
                pltpu.VMEM((tiles, n_chip, 8, TILE), F32),
                pltpu.VMEM((tiles, n_chip, 8, TILE), F32),
                pltpu.VMEM((tiles, 8, TILE), F32),
                pltpu.VMEM((creatives, TILE), F32),
                pltpu.VMEM((2, tiles, TILE), F32),
                pltpu.VMEM((own_tiles, block_lists.shape[1]), jnp.int32),
                pltpu.VMEM((2, 1, width), F32),
                pltpu.VMEM((n_chip, 1, TILE), F32),
                pltpu.VMEM((tiles, TILE), F32),
                pltpu.VMEM((tiles, TILE), F32),
                pltpu.VMEM((2, n_x, tiles, TILE), F32),
                pltpu.VMEM((2, own_tiles, TILE), F32),
                pltpu.VMEM((n_chip, n_chip // 2, TILE), F32),
                pltpu.VMEM((n_chip // 2, 1, TILE), F32),
                pltpu.VMEM((n_chip, 1, TILE), F32),
                pltpu.VMEM((2, n_chip // 2, TILE), F32),
                dma((6,)),
                dma((n_chip - 1,)),
                dma((n_chip,)),
                dma((n_chip,)),
                dma((n_chip,)),
                dma((2,)),
                dma((2,)),
                dma((2, n_x)),
                dma((2, n_x)),
                dma((2, n_chip)),
                dma((2, n_chip)),
            ],
            compiler_params=pltpu.CompilerParams(
                collective_id=0, has_side_effects=True, vmem_limit_bytes=63 << 20
            ),
        )(
            impressions,
            panels.reshape(width, wide),
            block_lists,
            block_counts,
            imp_weight.reshape(own_tiles, TILE),
            spend_goals,
            prices,
        )
        new_prices, spend, norms = pl.pallas_call(
            hand_on,
            out_shape=tuple(jax.ShapeDtypeStruct(x.shape, x.dtype) for x in results),
            in_specs=[any_spec] * 3,
            out_specs=(any_spec,) * 3,
            scratch_shapes=[dma((3,))],
            compiler_params=pltpu.CompilerParams(vmem_limit_bytes=63 << 20),
        )(*results)
        return new_prices, spend, norms.reshape(rows)

    return jax.shard_map(
        step,
        mesh=mesh,
        in_specs=(
            P("imp", None),
            P("cre", "imp", None),
            P("imp", None),
            P("imp"),
            P("imp"),
            P("cre", "imp"),
            P("cre", "imp"),
        ),
        out_specs=(P("cre", "imp"), P("cre", "imp"), P("imp")),
        check_vma=False,
    )
```

```python
import functools
import math

import jax
import jax.numpy as jnp
from jax import lax
from jax.experimental import pallas as pl
from jax.experimental.pallas import tpu as pltpu
from jax.sharding import PartitionSpec as P

MESH = pl.DeviceIdType.MESH
F32 = jnp.float32
TILE = 128
NEG_FILL = -1e30
TAU_INV = 4.0
STEP_RATE = 0.5
EXP2_SCALE = TAU_INV * math.log2(math.e)


def kernel(
    n_chip,
    n_cre,
    imp_hbm,
    panel_hbm,
    list_hbm,
    count_ref,
    weight_hbm,
    goal_hbm,
    price_hbm,
    new_price_ref,
    spend_ref,
    norm_ref,
    imps,
    panels,
    kmat,
    top,
    zsum,
    bias,
    factor,
    grow,
    vcol,
    wl,
    lists,
    pg_own,
    pg,
    mx_row,
    zt_row,
    lse,
    norms,
    part1,
    part2,
    got2,
    whole,
    local_sem,
    panel_send,
    panel_recv,
    pg_send,
    pg_recv,
    core_send,
    core_recv,
    x_send,
    x_recv,
    y_send,
    y_recv,
):
    i = lax.axis_index("imp")
    g = lax.axis_index("cre")
    c = lax.rem(i, 2)
    q = i // 2
    y = lax.rem(q, 2)
    z = q // 2
    nz = n_chip // 2
    half = nz // 2
    n_x = n_cre * 2
    me_x = g * 2 + c
    rows = imp_hbm.shape[0]
    width = panel_hbm.shape[0]
    tiles = 2 * rows // TILE
    own_tiles = tiles // 2
    packed = n_chip // 2

    mirror = g + 1 - 2 * lax.rem(g, 2)

    def plane(step):
        return lax.rem(z + step + nz, nz)

    def slot_of(step, dy):
        return plane(step) * 2 + (y if dy == 0 else 1 - y)

    def rel(step, dy):
        return step % nz * 2 + dy

    def at(step, dy):
        return {"imp": slot_of(step, dy) * 2 + c, "cre": g if dy == 0 else mirror}

    chips = [(half, 1), (half, 0)]
    for d in range(half - 1, 0, -1):
        chips += [(d, 1), (-d, 1), (d, 0), (-d, 0)]
    chips += [(0, 1)]

    x_half = n_cre // 4
    cres = [(x_half, dl, dc) for dl in (1, 0) for dc in (1, 0)]
    for d in range(x_half - 1, 0, -1):
        cres += [(s, dl, dc) for dl in (1, 0) for s in (d, -d) for dc in (1, 0)]
    cres += [(0, 1, 1), (0, 1, 0), (0, 0, 1)]

    def cre_slot(k):
        dx, dl, dc = cres[k - 1]
        line = lax.rem(g // 2 + dx + n_cre // 2, n_cre // 2)
        side = lax.rem(g + dl, 2)
        return line * 4 + side * 2 + lax.rem(c + dc, 2)

    def cre_peer(k):
        other = cre_slot(k)
        return {"imp": q * 2 + lax.rem(other, 2), "cre": other // 2}

    far_first = range(1, n_x)
    core_peer = {"imp": q * 2 + 1 - c, "cre": g}

    barrier = pltpu.get_barrier_semaphore()
    near = [(step, dy) for step, dy in chips if abs(step) <= 2]
    for step, dy in near:
        pl.semaphore_signal(barrier, inc=1, device_id=at(step, dy), device_id_type=MESH)
    for k in far_first:
        pl.semaphore_signal(barrier, inc=1, device_id=cre_peer(k), device_id_type=MESH)

    own_rows = pl.ds(pl.multiple_of(c * rows, rows), rows)

    def shard_ref(slot):
        return panels.at[pl.ds(slot * width, width)]

    local = [
        pltpu.make_async_copy(price_hbm, pg_own.at[0], local_sem.at[0]),
        pltpu.make_async_copy(goal_hbm, pg_own.at[1], local_sem.at[1]),
        pltpu.make_async_copy(list_hbm, lists, local_sem.at[2]),
        pltpu.make_async_copy(weight_hbm, wl.at[c, pl.ds(0, own_tiles)], local_sem.at[3]),
        pltpu.make_async_copy(panel_hbm, shard_ref(0), local_sem.at[4]),
        pltpu.make_async_copy(imp_hbm, imps.at[own_rows], local_sem.at[5]),
    ]
    for copy in local:
        copy.start()

    for copy in local[:2]:
        copy.wait()
    pg[0] = jnp.concatenate([pg_own[0], pg_own[1]], axis=1)
    pl.semaphore_wait(barrier, len(near) + n_x - 1)

    pg_copies = []

    def pg_copy(src, dst, peer, n=0):
        return pltpu.make_async_remote_copy(
            src_ref=pg.at[src],
            dst_ref=pg.at[dst],
            send_sem=pg_send.at[n],
            recv_sem=pg_recv.at[dst],
            device_id=peer,
            device_id_type=MESH,
        )

    def pg_put(src, dst, peer):
        copy = pg_copy(src, dst, peer, len(pg_copies))
        copy.start()
        pg_copies.append(copy)

    def pg_arrived(step, dy):
        pg_copy(0, rel(step, dy), at(0, 1)).wait_recv()

    for step, dy in near:
        pg_put(0, rel(-step, dy), at(step, dy))

    sent = []

    def panel_copy(src, slot, peer, n=0):
        return pltpu.make_async_remote_copy(
            src_ref=src,
            dst_ref=shard_ref(slot),
            send_sem=panel_send.at[n],
            recv_sem=panel_recv.at[slot],
            device_id=peer,
            device_id_type=MESH,
        )

    def send(src, slot, peer):
        copy = panel_copy(src, slot, peer, len(sent))
        copy.start()
        sent.append(copy)

    def arrived(step, dy):
        panel_copy(panel_hbm, rel(step, dy), at(0, 1)).wait_recv()

    for step in (2, -2, 1, -1):
        for dy in (1, 0):
            send(panel_hbm, rel(-step, dy), at(step, dy))
    send(panel_hbm, rel(0, 1), at(0, 1))

    imp_copy = pltpu.make_async_remote_copy(
        src_ref=imp_hbm,
        dst_ref=imps.at[own_rows],
        send_sem=core_send.at[1],
        recv_sem=core_recv.at[1],
        device_id=core_peer,
        device_id_type=MESH,
    )
    imp_copy.start()

    for copy in local[2:4]:
        copy.wait()
    sub = lax.broadcasted_iota(jnp.int32, lists.shape, 0)
    lane = lax.broadcasted_iota(jnp.int32, lists.shape, 1)
    counts = jnp.zeros(lists.shape, jnp.int32)
    for t in range(own_tiles):
        counts = jnp.where(sub == t, count_ref[t], counts)
    wl[c, pl.ds(own_tiles, own_tiles)] = jnp.full((own_tiles, TILE), -1.0, F32)
    wl[c, pl.ds(own_tiles, own_tiles), pl.ds(0, lists.shape[1])] = jnp.where(
        lane < counts, lists[...].astype(F32), -1.0
    )
    wl_copy = pltpu.make_async_remote_copy(
        src_ref=wl.at[c],
        dst_ref=wl.at[c],
        send_sem=core_send.at[0],
        recv_sem=core_recv.at[0],
        device_id=core_peer,
        device_id_type=MESH,
    )
    wl_copy.start()
    core_copies = [wl_copy, imp_copy]

    wl_copy.wait_recv()
    ids = lax.broadcasted_iota(jnp.int32, (n_chip, TILE), 0)
    same = lax.rem(ids, 2) == 0
    ids = lax.rem(lax.div(ids, 2) + z, nz) * 2
    ids = ids + jnp.where(same, g * n_chip + y, mirror * n_chip + 1 - y)
    ids = ids.astype(F32)
    for t in range(tiles):
        row = wl[t // own_tiles, own_tiles + t % own_tiles : own_tiles + t % own_tiles + 1, :]
        hit = jnp.max(jnp.where(row == ids, 1.0, 0.0), axis=1, keepdims=True)
        level = jnp.broadcast_to(jnp.where(hit > 0.0, 0.0, NEG_FILL), (n_chip, TILE))
        for b in range(n_chip):
            bias[t, b] = jnp.broadcast_to(level[b : b + 1, :], (8, TILE))

    for sign in (1, -1):
        for s in range(2):
            dy = s if sign == 1 else 1 - s
            slot = rel(-2 * sign, dy)
            pg_arrived(-2 * sign, dy)
            if s == 0:
                pg_put(slot, rel(half, dy), at(2 * sign, 0))
            pg_put(slot, rel(-3 * sign, dy), at(sign, 0))
            arrived(-2 * sign, dy)
            if s == 0:
                send(shard_ref(slot), rel(half, dy), at(2 * sign, 0))
            send(shard_ref(slot), rel(-3 * sign, dy), at(sign, 0))

    low = lax.broadcasted_iota(jnp.int32, (1, TILE), 1) < width
    def spread_row(d, row):
        v = jnp.exp(row)
        vcol[d * TILE : (d + 1) * TILE, :] = jnp.transpose(jnp.broadcast_to(v, (TILE, TILE)))
        return v

    def turned(row):
        return jnp.where(y == 0, row, pltpu.roll(row, width, 1))

    def plane_row(d):
        return pl.ds(plane(d), 1)

    values = {}

    def spread_slab(step):
        d = step % nz
        even, odd = pg[2 * d], pg[2 * d + 1]
        row = jnp.where(low, even, pltpu.roll(odd, width, 1))
        values[d] = spread_row(d, row)
        whole[0, plane_row(d), :] = turned(row)
        whole[1, plane_row(d), :] = turned(jnp.where(low, pltpu.roll(even, width, 1), odd))

    slab_rows = 2 * width

    def process(slabs):
        parts = []
        for zz in slabs:
            parts.append(panels[zz * slab_rows : (zz + 1) * slab_rows, :])
        pan = parts[0] if len(parts) == 1 else jnp.concatenate(parts, axis=0)

        def body(t2, carry):
            x = imps[pl.ds(pl.multiple_of(t2 * 2 * TILE, 2 * TILE), 2 * TILE), :]
            aff = lax.dot_general(pan, x, (((1,), (1,)), ((), ())), preferred_element_type=F32)
            for n, zz in enumerate(slabs):
                for h in range(2):
                    qq = zz * 2 + h
                    place = slice(qq * width, (qq + 1) * width)
                    v = vcol[place, :].reshape(width // 8, 8, TILE)
                    for side in range(2):
                        t = t2 * 2 + side
                        first = n * slab_rows + h * width
                        a = aff[first : first + width, side * TILE : (side + 1) * TILE]
                        a = a.reshape(width // 8, 8, TILE)
                        m = jnp.max(a, axis=0)
                        e = jnp.exp2((a - m) * EXP2_SCALE)
                        kmat[t, place, :] = e.reshape(width, TILE)
                        top[t, qq] = TAU_INV * m + bias[t, qq]
                        zsum[t, qq] = jnp.sum(e * v, axis=0)
            return carry

        lax.fori_loop(0, tiles // 2, body, 0, unroll=8)

    for copy in local[4:]:
        copy.wait()
    imp_copy.wait_recv()
    pg_arrived(0, 1)
    spread_slab(0)
    arrived(0, 1)
    process([0])
    for d in range(1, half):
        for step in (d, -d):
            for dy in range(2):
                if d != 2:
                    pg_arrived(step, dy)
            spread_slab(step)
        for step in (d, -d):
            for dy in range(2):
                if d != 2:
                    arrived(step, dy)
        if d + 1 < half:
            process([d, nz - d])
    for dy in range(2):
        pg_arrived(half, dy)
    spread_slab(half)
    for dy in range(2):
        arrived(half, dy)
    process([half - 1, half + 1, half])

    def drain(*groups):
        for group in groups:
            for copy in group:
                copy.wait_send()

    def exchange_norms(phase, earlier):
        lse[phase, me_x] = mx_row[...] + jnp.log(zt_row[...])
        copies = []
        for k in far_first:
            copy = pltpu.make_async_remote_copy(
                src_ref=lse.at[phase, me_x],
                dst_ref=lse.at[phase, me_x],
                send_sem=x_send.at[phase, k],
                recv_sem=x_recv.at[phase, me_x],
                device_id=cre_peer(k),
                device_id_type=MESH,
            )
            copy.start()
            copies.append(copy)
        drain(*earlier)
        for k in range(1, n_x):
            other = cre_slot(k)
            pltpu.make_async_remote_copy(
                src_ref=lse.at[phase, me_x],
                dst_ref=lse.at[phase, other],
                send_sem=x_send.at[phase, k],
                recv_sem=x_recv.at[phase, other],
                device_id=cre_peer(k),
                device_id_type=MESH,
            ).wait_recv()
        most = lse[phase, 0]
        for k in range(1, n_x):
            most = jnp.maximum(most, lse[phase, k])
        total = jnp.exp(lse[phase, 0] - most)
        for k in range(1, n_x):
            total = total + jnp.exp(lse[phase, k] - most)
        norm = most + jnp.log(total)
        norms[0] = norm[:own_tiles]
        norms[1] = norm[own_tiles:]
        weight = jnp.concatenate([wl[0, :own_tiles], wl[1, :own_tiles]], axis=0)
        gain = weight * jnp.exp(mx_row[...] - norm)
        for t in range(tiles):
            grow[t] = jnp.broadcast_to(gain[t : t + 1, :], (8, TILE))
        return copies

    def spends():
        ones = []
        for r in range(packed):

            def body(t, acc):
                gain = grow[t]
                out = []
                for h in range(2):
                    first = r * TILE + h * width
                    k = kmat[t, first : first + width, :].reshape(width // 8, 8, TILE)
                    out.append(acc[h] + k * (factor[t, 2 * r + h] * gain))
                return tuple(out)

            zero = jnp.zeros((width // 8, 8, TILE), F32)
            a0, a1 = lax.fori_loop(0, tiles, body, (zero, zero), unroll=tiles)
            both = jnp.concatenate([a0, a1], axis=0).reshape(TILE, TILE)
            ones.append(jnp.sum(jnp.transpose(both), axis=0, keepdims=True))
        return ones

    for t in range(tiles):
        lim = top[t]
        m = jnp.max(jnp.max(lim, axis=0), axis=0, keepdims=True)
        mx_row[t : t + 1, :] = m
        f = jnp.exp(lim - m)
        factor[t] = f
        zt_row[t : t + 1, :] = jnp.sum(jnp.sum(f * zsum[t], axis=0), axis=0, keepdims=True)
    x_copies = exchange_norms(0, (sent, core_copies, pg_copies))

    for d, value in enumerate(spends()):
        part1[q, plane_row(d), :] = turned(value * values[d])
    y_copies = []
    for k in range(n_chip - 1):
        copy = pltpu.make_async_remote_copy(
            src_ref=part1.at[q],
            dst_ref=part1.at[q],
            send_sem=y_send.at[0, k],
            recv_sem=y_recv.at[0, q],
            device_id=at(*chips[k]),
            device_id_type=MESH,
        )
        copy.start()
        y_copies.append(copy)
    drain(x_copies)
    for k in range(n_chip - 1):
        other = slot_of(*chips[k])
        pltpu.make_async_remote_copy(
            src_ref=part1.at[q],
            dst_ref=part1.at[other],
            send_sem=y_send.at[0, k],
            recv_sem=y_recv.at[0, other],
            device_id=at(*chips[k]),
            device_id_type=MESH,
        ).wait_recv()
    spend = part1[0]
    for k in range(1, n_chip):
        spend = spend + part1[k]
    goal = whole[1]
    whole[0] = whole[0] + STEP_RATE * (jnp.log(goal) - jnp.log(spend + 0.25 * goal))
    for d in range(nz):
        row = turned(whole[0, plane_row(d), :])
        values[d] = spread_row(d, row)
        if d == 0:
            price_row = row

    group = 4

    def zbody(n, carry):
        acc = [jnp.zeros((8, TILE), F32)] * group
        for b in range(n_chip):
            place = slice(b * width, (b + 1) * width)
            v = vcol[place, :].reshape(width // 8, 8, TILE)
            for m in range(group):
                t = n * group + m
                part = jnp.sum(kmat[t, place, :].reshape(width // 8, 8, TILE) * v, axis=0)
                acc[m] = acc[m] + part * factor[t, b]
        for m in range(group):
            zt_row[pl.ds(n * group + m, 1), :] = jnp.sum(acc[m], axis=0, keepdims=True)
        return carry

    lax.fori_loop(0, tiles // group, zbody, 0)
    x_last = exchange_norms(1, (y_copies,))

    for d, value in enumerate(spends()):
        part2[d] = value * values[d]

    def row_copy(step, dy, n):
        return pltpu.make_async_remote_copy(
            src_ref=part2.at[step % nz],
            dst_ref=got2.at[rel(-step, dy)],
            send_sem=y_send.at[1, n],
            recv_sem=y_recv.at[1, rel(-step, dy)],
            device_id=at(step, dy),
            device_id_type=MESH,
        )

    y_last = []
    for n, (step, dy) in enumerate(chips):
        copy = row_copy(step, dy, n)
        copy.start()
        y_last.append(copy)
    drain(x_last)
    got2[0] = part2[0]
    norm_ref[...] = norms[c]
    for step, dy in chips:
        row_copy(-step, dy, 0).wait_recv()
    sums = []
    for dy in range(2):
        total = got2[dy]
        for d in range(1, nz):
            total = total + got2[2 * d + dy]
        sums.append(total)
    spend = (sums[0] + pltpu.roll(sums[1], width, 1))[:, :width]
    goal = pg_own[1]
    change = jnp.log(goal) - jnp.log(spend + 0.25 * goal)
    spend_ref[...] = spend
    new_price_ref[...] = price_row[:, :width] + STEP_RATE * change

    drain(y_last)


def hand_on(price_ref, spend_ref, norm_ref, price_out, spend_out, norm_out, sem):
    pairs = ((price_ref, price_out), (spend_ref, spend_out), (norm_ref, norm_out))
    copies = [pltpu.make_async_copy(a, b, sem.at[n]) for n, (a, b) in enumerate(pairs)]
    for copy in copies:
        copy.start()
    for copy in copies:
        copy.wait()


def solution(mesh):
    n_chip = mesh.shape["imp"] // 2
    n_cre = mesh.shape["cre"]
    half = n_chip // 4

    def step(impressions, panels, block_lists, block_counts, imp_weight, spend_goals, prices):
        rows, wide = impressions.shape
        width = panels.shape[1]
        own_tiles = rows // TILE
        tiles = 2 * own_tiles
        n_x = n_cre * 2
        creatives = n_chip * width
        any_spec = pl.BlockSpec(memory_space=pl.ANY)
        vmem = pl.BlockSpec(memory_space=pltpu.VMEM)
        dma = pltpu.SemaphoreType.DMA
        results = pl.pallas_call(
            functools.partial(kernel, n_chip, n_cre),
            out_shape=(
                jax.ShapeDtypeStruct((1, width), F32),
                jax.ShapeDtypeStruct((1, width), F32),
                jax.ShapeDtypeStruct((own_tiles, TILE), F32),
            ),
            in_specs=[
                any_spec,
                any_spec,
                any_spec,
                pl.BlockSpec(memory_space=pltpu.SMEM),
                any_spec,
                any_spec,
                any_spec,
            ],
            out_specs=(vmem, vmem, vmem),
            scratch_shapes=[
                pltpu.VMEM((2 * rows, wide), jnp.bfloat16),
                pltpu.VMEM((creatives, wide), jnp.bfloat16),
                pltpu.VMEM((tiles, creatives, TILE), F32),
                pltpu.VMEM((tiles, n_chip, 8, TILE), F32),
                pltpu.VMEM((tiles, n_chip, 8, TILE), F32),
                pltpu.VMEM((tiles, n_chip, 8, TILE), F32),
                pltpu.VMEM((tiles, n_chip, 8, TILE), F32),
                pltpu.VMEM((tiles, 8, TILE), F32),
                pltpu.VMEM((creatives, TILE), F32),
                pltpu.VMEM((2, tiles, TILE), F32),
                pltpu.VMEM((own_tiles, block_lists.shape[1]), jnp.int32),
                pltpu.VMEM((2, 1, width), F32),
                pltpu.VMEM((n_chip, 1, TILE), F32),
                pltpu.VMEM((tiles, TILE), F32),
                pltpu.VMEM((tiles, TILE), F32),
                pltpu.VMEM((2, n_x, tiles, TILE), F32),
                pltpu.VMEM((2, own_tiles, TILE), F32),
                pltpu.VMEM((n_chip, n_chip // 2, TILE), F32),
                pltpu.VMEM((n_chip // 2, 1, TILE), F32),
                pltpu.VMEM((n_chip, 1, TILE), F32),
                pltpu.VMEM((2, n_chip // 2, TILE), F32),
                dma((6,)),
                dma((n_chip - 1,)),
                dma((n_chip,)),
                dma((n_chip,)),
                dma((n_chip,)),
                dma((2,)),
                dma((2,)),
                dma((2, n_x)),
                dma((2, n_x)),
                dma((2, n_chip)),
                dma((2, n_chip)),
            ],
            compiler_params=pltpu.CompilerParams(
                collective_id=0, has_side_effects=True, vmem_limit_bytes=63 << 20
            ),
        )(
            impressions,
            panels.reshape(width, wide),
            block_lists,
            block_counts,
            imp_weight.reshape(own_tiles, TILE),
            spend_goals,
            prices,
        )
        new_prices, spend, norms = pl.pallas_call(
            hand_on,
            out_shape=tuple(jax.ShapeDtypeStruct(x.shape, x.dtype) for x in results),
            in_specs=[any_spec] * 3,
            out_specs=(any_spec,) * 3,
            scratch_shapes=[dma((3,))],
            compiler_params=pltpu.CompilerParams(vmem_limit_bytes=63 << 20),
        )(*results)
        return new_prices, spend, norms.reshape(rows)

    return jax.shard_map(
        step,
        mesh=mesh,
        in_specs=(
            P("imp", None),
            P("cre", "imp", None),
            P("imp", None),
            P("imp"),
            P("imp"),
            P("cre", "imp"),
            P("cre", "imp"),
        ),
        out_specs=(P("cre", "imp"), P("cre", "imp"), P("imp")),
        check_vma=False,
    )
```

```python
import functools
import math

import jax
import jax.numpy as jnp
from jax import lax
from jax.experimental import pallas as pl
from jax.experimental.pallas import tpu as pltpu
from jax.sharding import PartitionSpec as P

MESH = pl.DeviceIdType.MESH
F32 = jnp.float32
TILE = 128
NEG_FILL = -1e30
TAU_INV = 4.0
STEP_RATE = 0.5
EXP2_SCALE = TAU_INV * math.log2(math.e)


def kernel(
    n_chip,
    n_cre,
    imp_hbm,
    panel_hbm,
    list_hbm,
    count_ref,
    weight_hbm,
    goal_hbm,
    price_hbm,
    new_price_ref,
    spend_ref,
    norm_ref,
    imps,
    panels,
    kmat,
    top,
    zsum,
    bias,
    factor,
    grow,
    vcol,
    wl,
    lists,
    pg_own,
    pg,
    mx_row,
    zt_row,
    lse,
    norms,
    part1,
    part2,
    got2,
    whole,
    local_sem,
    panel_send,
    panel_recv,
    pg_send,
    pg_recv,
    core_send,
    core_recv,
    x_send,
    x_recv,
    y_send,
    y_recv,
):
    i = lax.axis_index("imp")
    g = lax.axis_index("cre")
    c = lax.rem(i, 2)
    q = i // 2
    y = lax.rem(q, 2)
    z = q // 2
    nz = n_chip // 2
    half = nz // 2
    n_x = n_cre * 2
    me_x = g * 2 + c
    rows = imp_hbm.shape[0]
    width = panel_hbm.shape[0]
    tiles = 2 * rows // TILE
    own_tiles = tiles // 2
    packed = n_chip // 2

    mirror = g + 1 - 2 * lax.rem(g, 2)

    def plane(step):
        return lax.rem(z + step + nz, nz)

    def slot_of(step, dy):
        return plane(step) * 2 + (y if dy == 0 else 1 - y)

    def rel(step, dy):
        return step % nz * 2 + dy

    def at(step, dy):
        return {"imp": slot_of(step, dy) * 2 + c, "cre": g if dy == 0 else mirror}

    chips = [(half, 1), (half, 0)]
    for d in range(half - 1, 0, -1):
        chips += [(d, 1), (-d, 1), (d, 0), (-d, 0)]
    chips += [(0, 1)]

    x_half = n_cre // 4
    cres = [(x_half, dl, dc) for dl in (1, 0) for dc in (1, 0)]
    for d in range(x_half - 1, 0, -1):
        cres += [(s, dl, dc) for dl in (1, 0) for s in (d, -d) for dc in (1, 0)]
    cres += [(0, 1, 1), (0, 1, 0), (0, 0, 1)]

    def cre_slot(k):
        dx, dl, dc = cres[k - 1]
        line = lax.rem(g // 2 + dx + n_cre // 2, n_cre // 2)
        side = lax.rem(g + dl, 2)
        return line * 4 + side * 2 + lax.rem(c + dc, 2)

    def cre_peer(k):
        other = cre_slot(k)
        return {"imp": q * 2 + lax.rem(other, 2), "cre": other // 2}

    far_first = range(1, n_x)
    core_peer = {"imp": q * 2 + 1 - c, "cre": g}

    own_rows = pl.ds(pl.multiple_of(c * rows, rows), rows)

    def shard_ref(slot):
        return panels.at[pl.ds(slot * width, width)]

    local = [
        pltpu.make_async_copy(price_hbm, pg_own.at[0], local_sem.at[0]),
        pltpu.make_async_copy(goal_hbm, pg_own.at[1], local_sem.at[1]),
        pltpu.make_async_copy(list_hbm, lists, local_sem.at[2]),
        pltpu.make_async_copy(weight_hbm, wl.at[c, pl.ds(0, own_tiles)], local_sem.at[3]),
        pltpu.make_async_copy(panel_hbm, shard_ref(0), local_sem.at[4]),
        pltpu.make_async_copy(imp_hbm, imps.at[own_rows], local_sem.at[5]),
    ]
    for copy in local[:2]:
        copy.start()

    barrier = pltpu.get_barrier_semaphore()
    near = [(step, dy) for step, dy in chips if abs(step) <= 2]
    for step, dy in near:
        pl.semaphore_signal(barrier, inc=1, device_id=at(step, dy), device_id_type=MESH)
    for k in far_first:
        pl.semaphore_signal(barrier, inc=1, device_id=cre_peer(k), device_id_type=MESH)

    for copy in local[2:]:
        copy.start()

    for copy in local[:2]:
        copy.wait()
    pg[0] = jnp.concatenate([pg_own[0], pg_own[1]], axis=1)
    pl.semaphore_wait(barrier, len(near) + n_x - 1)

    pg_copies = []

    def pg_copy(src, dst, peer, n=0):
        return pltpu.make_async_remote_copy(
            src_ref=pg.at[src],
            dst_ref=pg.at[dst],
            send_sem=pg_send.at[n],
            recv_sem=pg_recv.at[dst],
            device_id=peer,
            device_id_type=MESH,
        )

    def pg_put(src, dst, peer):
        copy = pg_copy(src, dst, peer, len(pg_copies))
        copy.start()
        pg_copies.append(copy)

    def pg_arrived(step, dy):
        pg_copy(0, rel(step, dy), at(0, 1)).wait_recv()

    for step, dy in near:
        pg_put(0, rel(-step, dy), at(step, dy))

    sent = []

    def panel_copy(src, slot, peer, n=0):
        return pltpu.make_async_remote_copy(
            src_ref=src,
            dst_ref=shard_ref(slot),
            send_sem=panel_send.at[n],
            recv_sem=panel_recv.at[slot],
            device_id=peer,
            device_id_type=MESH,
        )

    def send(src, slot, peer):
        copy = panel_copy(src, slot, peer, len(sent))
        copy.start()
        sent.append(copy)

    def arrived(step, dy):
        panel_copy(panel_hbm, rel(step, dy), at(0, 1)).wait_recv()

    for step in (2, -2, 1, -1):
        for dy in (1, 0):
            send(panel_hbm, rel(-step, dy), at(step, dy))
    send(panel_hbm, rel(0, 1), at(0, 1))

    imp_copy = pltpu.make_async_remote_copy(
        src_ref=imp_hbm,
        dst_ref=imps.at[own_rows],
        send_sem=core_send.at[1],
        recv_sem=core_recv.at[1],
        device_id=core_peer,
        device_id_type=MESH,
    )
    imp_copy.start()

    for copy in local[2:4]:
        copy.wait()
    sub = lax.broadcasted_iota(jnp.int32, lists.shape, 0)
    lane = lax.broadcasted_iota(jnp.int32, lists.shape, 1)
    counts = jnp.zeros(lists.shape, jnp.int32)
    for t in range(own_tiles):
        counts = jnp.where(sub == t, count_ref[t], counts)
    wl[c, pl.ds(own_tiles, own_tiles)] = jnp.full((own_tiles, TILE), -1.0, F32)
    wl[c, pl.ds(own_tiles, own_tiles), pl.ds(0, lists.shape[1])] = jnp.where(
        lane < counts, lists[...].astype(F32), -1.0
    )
    wl_copy = pltpu.make_async_remote_copy(
        src_ref=wl.at[c],
        dst_ref=wl.at[c],
        send_sem=core_send.at[0],
        recv_sem=core_recv.at[0],
        device_id=core_peer,
        device_id_type=MESH,
    )
    wl_copy.start()
    core_copies = [wl_copy, imp_copy]

    wl_copy.wait_recv()
    ids = lax.broadcasted_iota(jnp.int32, (n_chip, TILE), 0)
    same = lax.rem(ids, 2) == 0
    ids = lax.rem(lax.div(ids, 2) + z, nz) * 2
    ids = ids + jnp.where(same, g * n_chip + y, mirror * n_chip + 1 - y)
    ids = ids.astype(F32)
    for t in range(tiles):
        row = wl[t // own_tiles, own_tiles + t % own_tiles : own_tiles + t % own_tiles + 1, :]
        hit = jnp.max(jnp.where(row == ids, 1.0, 0.0), axis=1, keepdims=True)
        level = jnp.broadcast_to(jnp.where(hit > 0.0, 0.0, NEG_FILL), (n_chip, TILE))
        for b in range(n_chip):
            bias[t, b] = jnp.broadcast_to(level[b : b + 1, :], (8, TILE))

    for sign in (1, -1):
        for s in range(2):
            dy = s if sign == 1 else 1 - s
            slot = rel(-2 * sign, dy)
            pg_arrived(-2 * sign, dy)
            if s == 0:
                pg_put(slot, rel(half, dy), at(2 * sign, 0))
            pg_put(slot, rel(-3 * sign, dy), at(sign, 0))
            arrived(-2 * sign, dy)
            if s == 0:
                send(shard_ref(slot), rel(half, dy), at(2 * sign, 0))
            send(shard_ref(slot), rel(-3 * sign, dy), at(sign, 0))

    low = lax.broadcasted_iota(jnp.int32, (1, TILE), 1) < width
    def spread_row(d, row):
        v = jnp.exp(row)
        vcol[d * TILE : (d + 1) * TILE, :] = jnp.transpose(jnp.broadcast_to(v, (TILE, TILE)))
        return v

    def turned(row):
        return jnp.where(y == 0, row, pltpu.roll(row, width, 1))

    def plane_row(d):
        return pl.ds(plane(d), 1)

    values = {}

    def spread_slab(step):
        d = step % nz
        even, odd = pg[2 * d], pg[2 * d + 1]
        row = jnp.where(low, even, pltpu.roll(odd, width, 1))
        values[d] = spread_row(d, row)
        whole[0, plane_row(d), :] = turned(row)
        whole[1, plane_row(d), :] = turned(jnp.where(low, pltpu.roll(even, width, 1), odd))

    slab_rows = 2 * width

    def process(slabs):
        parts = []
        for zz in slabs:
            parts.append(panels[zz * slab_rows : (zz + 1) * slab_rows, :])
        pan = parts[0] if len(parts) == 1 else jnp.concatenate(parts, axis=0)

        def body(t2, carry):
            x = imps[pl.ds(pl.multiple_of(t2 * 2 * TILE, 2 * TILE), 2 * TILE), :]
            aff = lax.dot_general(pan, x, (((1,), (1,)), ((), ())), preferred_element_type=F32)
            for n, zz in enumerate(slabs):
                for h in range(2):
                    qq = zz * 2 + h
                    place = slice(qq * width, (qq + 1) * width)
                    v = vcol[place, :].reshape(width // 8, 8, TILE)
                    for side in range(2):
                        t = t2 * 2 + side
                        first = n * slab_rows + h * width
                        a = aff[first : first + width, side * TILE : (side + 1) * TILE]
                        a = a.reshape(width // 8, 8, TILE)
                        m = jnp.max(a, axis=0)
                        e = jnp.exp2((a - m) * EXP2_SCALE)
                        kmat[t, place, :] = e.reshape(width, TILE)
                        top[t, qq] = TAU_INV * m + bias[t, qq]
                        zsum[t, qq] = jnp.sum(e * v, axis=0)
            return carry

        lax.fori_loop(0, tiles // 2, body, 0, unroll=8)

    for copy in local[4:]:
        copy.wait()
    imp_copy.wait_recv()
    pg_arrived(0, 1)
    spread_slab(0)
    arrived(0, 1)
    process([0])
    for d in range(1, half):
        for step in (d, -d):
            for dy in range(2):
                if d != 2:
                    pg_arrived(step, dy)
            spread_slab(step)
        for step in (d, -d):
            for dy in range(2):
                if d != 2:
                    arrived(step, dy)
        if d + 1 < half:
            process([d, nz - d])
    for dy in range(2):
        pg_arrived(half, dy)
    spread_slab(half)
    for dy in range(2):
        arrived(half, dy)
    process([half - 1, half + 1, half])

    def drain(*groups):
        for group in groups:
            for copy in group:
                copy.wait_send()

    def exchange_norms(phase, earlier):
        lse[phase, me_x] = mx_row[...] + jnp.log(zt_row[...])
        copies = []
        for k in far_first:
            copy = pltpu.make_async_remote_copy(
                src_ref=lse.at[phase, me_x],
                dst_ref=lse.at[phase, me_x],
                send_sem=x_send.at[phase, k],
                recv_sem=x_recv.at[phase, me_x],
                device_id=cre_peer(k),
                device_id_type=MESH,
            )
            copy.start()
            copies.append(copy)
        drain(*earlier)
        for k in range(1, n_x):
            other = cre_slot(k)
            pltpu.make_async_remote_copy(
                src_ref=lse.at[phase, me_x],
                dst_ref=lse.at[phase, other],
                send_sem=x_send.at[phase, k],
                recv_sem=x_recv.at[phase, other],
                device_id=cre_peer(k),
                device_id_type=MESH,
            ).wait_recv()
        most = lse[phase, 0]
        for k in range(1, n_x):
            most = jnp.maximum(most, lse[phase, k])
        total = jnp.exp(lse[phase, 0] - most)
        for k in range(1, n_x):
            total = total + jnp.exp(lse[phase, k] - most)
        norm = most + jnp.log(total)
        norms[0] = norm[:own_tiles]
        norms[1] = norm[own_tiles:]
        weight = jnp.concatenate([wl[0, :own_tiles], wl[1, :own_tiles]], axis=0)
        gain = weight * jnp.exp(mx_row[...] - norm)
        for t in range(tiles):
            grow[t] = jnp.broadcast_to(gain[t : t + 1, :], (8, TILE))
        return copies

    def spends():
        ones = []
        for r in range(packed):

            def body(t, acc):
                gain = grow[t]
                out = []
                for h in range(2):
                    first = r * TILE + h * width
                    k = kmat[t, first : first + width, :].reshape(width // 8, 8, TILE)
                    out.append(acc[h] + k * (factor[t, 2 * r + h] * gain))
                return tuple(out)

            zero = jnp.zeros((width // 8, 8, TILE), F32)
            a0, a1 = lax.fori_loop(0, tiles, body, (zero, zero), unroll=tiles)
            both = jnp.concatenate([a0, a1], axis=0).reshape(TILE, TILE)
            ones.append(jnp.sum(jnp.transpose(both), axis=0, keepdims=True))
        return ones

    for t in range(tiles):
        lim = top[t]
        m = jnp.max(jnp.max(lim, axis=0), axis=0, keepdims=True)
        mx_row[t : t + 1, :] = m
        f = jnp.exp(lim - m)
        factor[t] = f
        zt_row[t : t + 1, :] = jnp.sum(jnp.sum(f * zsum[t], axis=0), axis=0, keepdims=True)
    x_copies = exchange_norms(0, (sent, core_copies, pg_copies))

    for d, value in enumerate(spends()):
        part1[q, plane_row(d), :] = turned(value * values[d])
    y_copies = []
    for k in range(n_chip - 1):
        copy = pltpu.make_async_remote_copy(
            src_ref=part1.at[q],
            dst_ref=part1.at[q],
            send_sem=y_send.at[0, k],
            recv_sem=y_recv.at[0, q],
            device_id=at(*chips[k]),
            device_id_type=MESH,
        )
        copy.start()
        y_copies.append(copy)
    drain(x_copies)
    for k in range(n_chip - 1):
        other = slot_of(*chips[k])
        pltpu.make_async_remote_copy(
            src_ref=part1.at[q],
            dst_ref=part1.at[other],
            send_sem=y_send.at[0, k],
            recv_sem=y_recv.at[0, other],
            device_id=at(*chips[k]),
            device_id_type=MESH,
        ).wait_recv()
    spend = part1[0]
    for k in range(1, n_chip):
        spend = spend + part1[k]
    goal = whole[1]
    whole[0] = whole[0] + STEP_RATE * (jnp.log(goal) - jnp.log(spend + 0.25 * goal))
    for d in range(nz):
        row = turned(whole[0, plane_row(d), :])
        values[d] = spread_row(d, row)
        if d == 0:
            price_row = row

    group = 4

    def zbody(n, carry):
        acc = [jnp.zeros((8, TILE), F32)] * group
        for b in range(n_chip):
            place = slice(b * width, (b + 1) * width)
            v = vcol[place, :].reshape(width // 8, 8, TILE)
            for m in range(group):
                t = n * group + m
                part = jnp.sum(kmat[t, place, :].reshape(width // 8, 8, TILE) * v, axis=0)
                acc[m] = acc[m] + part * factor[t, b]
        for m in range(group):
            zt_row[pl.ds(n * group + m, 1), :] = jnp.sum(acc[m], axis=0, keepdims=True)
        return carry

    lax.fori_loop(0, tiles // group, zbody, 0)
    x_last = exchange_norms(1, (y_copies,))

    for d, value in enumerate(spends()):
        part2[d] = value * values[d]

    def row_copy(step, dy, n):
        return pltpu.make_async_remote_copy(
            src_ref=part2.at[step % nz],
            dst_ref=got2.at[rel(-step, dy)],
            send_sem=y_send.at[1, n],
            recv_sem=y_recv.at[1, rel(-step, dy)],
            device_id=at(step, dy),
            device_id_type=MESH,
        )

    y_last = []
    for n, (step, dy) in enumerate(chips):
        copy = row_copy(step, dy, n)
        copy.start()
        y_last.append(copy)
    drain(x_last)
    got2[0] = part2[0]
    norm_ref[...] = norms[c]
    for step, dy in chips:
        row_copy(-step, dy, 0).wait_recv()
    sums = []
    for dy in range(2):
        total = got2[dy]
        for d in range(1, nz):
            total = total + got2[2 * d + dy]
        sums.append(total)
    spend = (sums[0] + pltpu.roll(sums[1], width, 1))[:, :width]
    goal = pg_own[1]
    change = jnp.log(goal) - jnp.log(spend + 0.25 * goal)
    spend_ref[...] = spend
    new_price_ref[...] = price_row[:, :width] + STEP_RATE * change

    drain(y_last)


def hand_on(price_ref, spend_ref, norm_ref, price_out, spend_out, norm_out, sem):
    pairs = ((price_ref, price_out), (spend_ref, spend_out), (norm_ref, norm_out))
    copies = [pltpu.make_async_copy(a, b, sem.at[n]) for n, (a, b) in enumerate(pairs)]
    for copy in copies:
        copy.start()
    for copy in copies:
        copy.wait()


def solution(mesh):
    n_chip = mesh.shape["imp"] // 2
    n_cre = mesh.shape["cre"]
    half = n_chip // 4

    def step(impressions, panels, block_lists, block_counts, imp_weight, spend_goals, prices):
        rows, wide = impressions.shape
        width = panels.shape[1]
        own_tiles = rows // TILE
        tiles = 2 * own_tiles
        n_x = n_cre * 2
        creatives = n_chip * width
        any_spec = pl.BlockSpec(memory_space=pl.ANY)
        vmem = pl.BlockSpec(memory_space=pltpu.VMEM)
        dma = pltpu.SemaphoreType.DMA
        results = pl.pallas_call(
            functools.partial(kernel, n_chip, n_cre),
            out_shape=(
                jax.ShapeDtypeStruct((1, width), F32),
                jax.ShapeDtypeStruct((1, width), F32),
                jax.ShapeDtypeStruct((own_tiles, TILE), F32),
            ),
            in_specs=[
                any_spec,
                any_spec,
                any_spec,
                pl.BlockSpec(memory_space=pltpu.SMEM),
                any_spec,
                any_spec,
                any_spec,
            ],
            out_specs=(vmem, vmem, vmem),
            scratch_shapes=[
                pltpu.VMEM((2 * rows, wide), jnp.bfloat16),
                pltpu.VMEM((creatives, wide), jnp.bfloat16),
                pltpu.VMEM((tiles, creatives, TILE), F32),
                pltpu.VMEM((tiles, n_chip, 8, TILE), F32),
                pltpu.VMEM((tiles, n_chip, 8, TILE), F32),
                pltpu.VMEM((tiles, n_chip, 8, TILE), F32),
                pltpu.VMEM((tiles, n_chip, 8, TILE), F32),
                pltpu.VMEM((tiles, 8, TILE), F32),
                pltpu.VMEM((creatives, TILE), F32),
                pltpu.VMEM((2, tiles, TILE), F32),
                pltpu.VMEM((own_tiles, block_lists.shape[1]), jnp.int32),
                pltpu.VMEM((2, 1, width), F32),
                pltpu.VMEM((n_chip, 1, TILE), F32),
                pltpu.VMEM((tiles, TILE), F32),
                pltpu.VMEM((tiles, TILE), F32),
                pltpu.VMEM((2, n_x, tiles, TILE), F32),
                pltpu.VMEM((2, own_tiles, TILE), F32),
                pltpu.VMEM((n_chip, n_chip // 2, TILE), F32),
                pltpu.VMEM((n_chip // 2, 1, TILE), F32),
                pltpu.VMEM((n_chip, 1, TILE), F32),
                pltpu.VMEM((2, n_chip // 2, TILE), F32),
                dma((6,)),
                dma((n_chip - 1,)),
                dma((n_chip,)),
                dma((n_chip,)),
                dma((n_chip,)),
                dma((2,)),
                dma((2,)),
                dma((2, n_x)),
                dma((2, n_x)),
                dma((2, n_chip)),
                dma((2, n_chip)),
            ],
            compiler_params=pltpu.CompilerParams(
                collective_id=0, has_side_effects=True, vmem_limit_bytes=63 << 20
            ),
        )(
            impressions,
            panels.reshape(width, wide),
            block_lists,
            block_counts,
            imp_weight.reshape(own_tiles, TILE),
            spend_goals,
            prices,
        )
        new_prices, spend, norms = pl.pallas_call(
            hand_on,
            out_shape=tuple(jax.ShapeDtypeStruct(x.shape, x.dtype) for x in results),
            in_specs=[any_spec] * 3,
            out_specs=(any_spec,) * 3,
            scratch_shapes=[dma((3,))],
            compiler_params=pltpu.CompilerParams(vmem_limit_bytes=63 << 20),
        )(*results)
        return new_prices, spend, norms.reshape(rows)

    return jax.shard_map(
        step,
        mesh=mesh,
        in_specs=(
            P("imp", None),
            P("cre", "imp", None),
            P("imp", None),
            P("imp"),
            P("imp"),
            P("cre", "imp"),
            P("cre", "imp"),
        ),
        out_specs=(P("cre", "imp"), P("cre", "imp"), P("imp")),
        check_vma=False,
    )
```
